1024 devices in a mesh: gx: 64 (over z, y), gy: 16 (over x, core).
Axes of the slice: x: 8, y: 8, z: 8, core: 2. Of those that a mesh axis runs over, the one named last changes fastest.
Arguments:
- adjoint_trace: bfloat16 [1024, 256, 16, 128], P('gx', 'gy'), may hold values from -6 to 6
- coupling: bfloat16 [7, 128, 128], replicated, may hold values from -0.1875 to 0.1875
- log_friction: float32 [512, 256, 128], P('gx', 'gy'), may hold values from -1 to 1
- send_column: int32 [64, 16, 256], P('gx', 'gy'), may hold values from 0 to 255, each once within a row
- live_count: int32 [64, 16, 16], P('gx', 'gy'), may hold values from 0 to 16, as said below
- target_node: int32 [64, 16, 16, 16], P('gx', 'gy'), may hold values from 0 to 127
Outputs:
- trace_update: bfloat16 [1024, 256, 16, 128], P('gx', 'gy')
- friction_gradient: float32 [512, 256, 128], P('gx', 'gy')
The draws below stay inside these ranges and needn't reach their ends.
Inputs may be any that keep to these rules, and one draw needn't show every extreme that they name: Each row of send_column lists every local basal face once. `live_count`: in every row of devices along gy, one owner receives 16 live blocks from every device.
All inputs are finite; a program needn't handle non-finite values.
Results may differ from the reference program's by a relative error of at most 0.0059.
Values may be sent and summed in bfloat16 or wider, within the bound.
No kernel may reach another device: no remote copies, remote signals or barrier semaphores. Data moves between devices by JAX's collectives and lax.ppermute only.
A program may use at most 32 MiB of HBM per device.

```python
import jax
import jax.numpy as jnp
from jax import lax

TRACE = 128
CX = 16
CY = 16
LAYERS = 16
PX = 8
PY = 16
NB = 256
CAP = 16
NX = 1024
NY = 256
MX = 512
MY = 256
N_GX = 64
N_GY = 16


def draw_live_count(key, part):
    first, second, third = jax.random.split(key, 3)
    base = jax.random.randint(first, (N_GX, N_GY, N_GY), 0, CAP + 1)
    level = jax.random.randint(second, (N_GX, N_GY, 1), 1, 5)
    counted = jnp.minimum(base * level // 2, CAP)
    full_owner = jax.random.randint(third, (N_GX, 1, 1), 0, N_GY)
    owners = jnp.arange(N_GY)[None, None, :]
    return jnp.where(owners == full_owner, CAP, counted).astype(jnp.int32)


def set_ends(array, own_key, low, top_value):
    extent = array.shape
    spot = [jax.random.randint(jax.random.fold_in(own_key, axis), (), 0, extent[axis]) for axis in range(len(extent))]
    array = array.at[tuple(spot)].set(low)
    longest = extent.index(max(extent))
    spot[longest] = (spot[longest] + 1) % extent[longest]
    return array.at[tuple(spot)].set(top_value)


def level_of(key, extent, shards, smallest, largest):
    def one(dim, shards_of):
        heights = jax.random.uniform(jax.random.fold_in(jax.random.fold_in(key, 6), dim), (shards_of,), jnp.float32, smallest / len(shards), largest / len(shards))
        return jnp.repeat(jnp.exp(heights), extent[dim] // shards_of).reshape((-1,) + (1,) * (len(extent) - dim - 1))

    factor_of = one(*shards[0])
    for cut in shards[1:]:
        factor_of = factor_of * one(*cut)
    return factor_of


def scatter_about(rng, shape, deviation, most, shards=(), held_as=jnp.bfloat16):
    entries = jax.random.normal(rng, shape, jnp.float32) * deviation
    if len(shards) > 0:
        entries = level_of(rng, shape, shards, -0.22, 0.18) * entries
    return jnp.clip(entries, min=-most, max=most).astype(held_as)


def setup_inputs(seed: int = 0) -> dict:
    key_list = jax.random.split(jax.random.key(seed), 7)
    adjoint_trace = scatter_about(key_list[0], (NX, NY, LAYERS, TRACE), 1.0, 6.0, ((0, 64), (1, 16)))
    coupling = scatter_about(key_list[1], (7, TRACE, TRACE), (7 * TRACE) ** -0.5, 0.1875)
    log_friction = jnp.clip(jax.random.uniform(key_list[2], (MX, MY, TRACE), jnp.float32, -1.0, 1.0) * level_of(key_list[2], (MX, MY, TRACE), ((0, 64), (1, 16)), -0.4, 0.0), -1.0, 1.0)
    send_column = jax.vmap(lambda own: jax.random.permutation(own, NB))(jax.random.split(key_list[3], N_GX * N_GY)).reshape((N_GX, N_GY, NB)).astype(jnp.int32)
    live_count = draw_live_count(jax.random.fold_in(key_list[6], 71), 0)
    target_node = set_ends(jax.random.randint(key_list[5], (N_GX, N_GY, N_GY, CAP), 0, PX * PY), jax.random.fold_in(key_list[5], 1), 0, (PX * PY) - 1).astype(jnp.int32)
    return {"adjoint_trace": adjoint_trace, "coupling": coupling, "log_friction": log_friction, "send_column": send_column, "live_count": live_count, "target_node": target_node}


def couple(extended, coupling):
    own = extended[1:-1, 1:-1]
    rows_a, rows_b, layers_n, width = own.shape
    zeros_layer = jnp.zeros((rows_a, rows_b, 1, width), jnp.bfloat16)
    below = jnp.concatenate([zeros_layer, own[:, :, :-1]], axis=2)
    above = jnp.concatenate([own[:, :, 1:], zeros_layer], axis=2)
    terms = [own, below, above, extended[:-2, 1:-1], extended[2:, 1:-1], extended[1:-1, :-2], extended[1:-1, 2:]]
    total = jnp.zeros((rows_a * rows_b * layers_n, width), jnp.float32)
    for index in range(7):
        total = total + jnp.dot(terms[index].reshape(-1, width), coupling[index], preferred_element_type=jnp.float32)
    return total.reshape(rows_a, rows_b, layers_n, width).astype(jnp.bfloat16)


def stencil(extended):
    center = extended[1:-1, 1:-1]
    beside_all = extended[2:, 1:-1] + extended[:-2, 1:-1] + extended[1:-1, 2:] + extended[1:-1, :-2]
    return 1.3 * center - 0.2 * beside_all


def reference(adjoint_trace, coupling, log_friction, send_column, live_count, target_node):
    padded = jnp.pad(adjoint_trace, ((1, 1), (1, 1), (0, 0), (0, 0)))

    def slab(index):
        extended = lax.dynamic_slice_in_dim(padded, index * CX, CX + 2, 0)
        return couple(extended, coupling)

    trace_update = lax.map(slab, jnp.arange(N_GX).astype(jnp.int32)).reshape(NX, NY, LAYERS, TRACE)
    bottom = trace_update[:, :, 0, :]
    local_faces = bottom.reshape(N_GX, CX, N_GY, CY, TRACE).transpose(0, 2, 1, 3, 4).reshape(N_GX, N_GY, NB, TRACE)
    picked = jnp.take_along_axis(local_faces, send_column[:, :, :, None], axis=2)
    picked = picked.reshape(N_GX, N_GY, N_GY, CAP, TRACE)
    live = jnp.arange(CAP).astype(jnp.int32)[None, None, None, :] < live_count[:, :, :, None]
    tile_nodes = PX * PY
    row_ids = (jnp.arange(N_GX).astype(jnp.int32)[:, None, None, None] * (N_GY * tile_nodes)
               + jnp.arange(N_GY).astype(jnp.int32)[None, None, :, None] * tile_nodes + target_node)
    dump_row = N_GX * N_GY * tile_nodes
    ids = jnp.where(live, row_ids, dump_row).reshape(-1).astype(jnp.int32)
    misfit = jax.ops.segment_sum(picked.reshape(-1, TRACE).astype(jnp.float32), ids, num_segments=dump_row + 1)[:dump_row]
    misfit = misfit.reshape(N_GX, N_GY, PX, PY, TRACE).transpose(0, 2, 1, 3, 4).reshape(MX, MY, TRACE)
    once = stencil(jnp.pad(log_friction, ((1, 1), (1, 1), (0, 0))))
    prior = stencil(jnp.pad(once, ((1, 1), (1, 1), (0, 0))))
    friction_gradient = jnp.exp(log_friction) * misfit + prior
    return trace_update, friction_gradient
```

```python
import functools

import jax
import jax.numpy as jnp
from jax import lax
from jax.experimental import pallas as pl
from jax.experimental.pallas import tpu as pltpu
from jax.sharding import PartitionSpec as P

F32 = jnp.float32
BF16 = jnp.bfloat16
VMEM = pl.BlockSpec(memory_space=pltpu.VMEM)
ANY = pl.BlockSpec(memory_space=pl.ANY)
MSG = 24


def dot(a, b):
    return jnp.dot(a, b, preferred_element_type=F32)


def shift(block, axis, step):
    count = lax.axis_size(axis)
    pairs = [(i, i + step) for i in range(count) if 0 <= i + step < count]
    return lax.ppermute(block, axis, pairs)


def pack_body(adj, logf, to_a_hi, to_a_lo, to_b_hi, to_b_lo, sems):
    ca, cb = adj.shape[0], adj.shape[1]
    pa, pb = logf.shape[0], logf.shape[1]
    copies = [
        pltpu.make_async_copy(adj.at[ca - 1], to_a_hi.at[pl.ds(0, cb)], sems.at[0]),
        pltpu.make_async_copy(adj.at[0], to_a_lo.at[pl.ds(0, cb)], sems.at[1]),
        pltpu.make_async_copy(adj.at[:, cb - 1], to_b_hi.at[pl.ds(0, ca)], sems.at[2]),
        pltpu.make_async_copy(adj.at[:, 0], to_b_lo.at[pl.ds(0, ca)], sems.at[3]),
    ]
    for copy in copies:
        copy.start()
    to_a_hi[cb:cb + 2] = logf[pa - 2:pa].astype(BF16)
    to_a_lo[cb:cb + 2] = logf[0:2].astype(BF16)
    to_b_hi[ca] = jnp.concatenate([logf[:, pb - 2, :], logf[:, pb - 1, :]], axis=0).astype(BF16)
    to_b_lo[ca] = jnp.concatenate([logf[:, 0, :], logf[:, 1, :]], axis=0).astype(BF16)
    for copy in copies:
        copy.wait()


def local_body(adj, coupling, send, live, nodes, base, pick, ids, wide):
    ca, cb, nl, width = adj.shape
    faces = ca * cb
    for a in range(ca):
        wide[a * cb * 8:(a + 1) * cb * 8] = adj[a, :, 0:8, :].astype(F32).reshape(cb * 8, width)
    low = wide[pl.ds(0, faces, stride=8), :].astype(BF16)
    above = wide[pl.ds(1, faces, stride=8), :].astype(BF16)
    total = dot(low, coupling[0]) + dot(above, coupling[2])
    zeros = jnp.zeros((cb, width), F32)
    total = total + jnp.concatenate([zeros, dot(low[:faces - cb], coupling[3])], axis=0)
    total = total + jnp.concatenate([dot(low[cb:], coupling[4]), zeros], axis=0)
    column = lax.broadcasted_iota(jnp.int32, (faces, width), 0) % cb
    before = pltpu.roll(dot(low, coupling[5]), 1, 0)
    after = pltpu.roll(dot(low, coupling[6]), faces - 1, 0)
    total = total + jnp.where(column > 0, before, 0.0) + jnp.where(column < cb - 1, after, 0.0)
    base[...] = total
    face = lax.broadcasted_iota(jnp.int32, (faces, faces), 0)
    picked_by = jnp.where(send[0] == face, 1.0, 0.0)
    pick[...] = picked_by.T.astype(BF16)
    owners, slots = nodes.shape[2], nodes.shape[3]
    sub = lax.broadcasted_iota(jnp.int32, (slots, width), 0)
    lane = lax.broadcasted_iota(jnp.int32, (slots, width), 1)
    spread = jnp.where(lane % slots == sub, 1.0, 0.0).astype(BF16)
    listed = dot(nodes[0, 0].astype(F32).astype(BF16), spread) + 1.0
    owner = lax.broadcasted_iota(jnp.int32, (owners, owners), 0)
    other = lax.broadcasted_iota(jnp.int32, (owners, owners), 1)
    counts = jnp.sum(jnp.where(owner == other, live[0].astype(F32), 0.0), axis=1, keepdims=True)
    lane = lax.broadcasted_iota(jnp.int32, (owners, width), 1)
    mine = lane // slots == lax.axis_index("gy") % (width // slots)
    alive = (lane % slots).astype(F32) < counts
    ids[...] = jnp.where(jnp.logical_and(mine, alive), listed, 0.0)


def message_body(base, pick, ids, coupling, a_lo, a_hi, b_lo, b_hi, out, total, wide):
    faces, width = base.shape
    owners, slots = out.shape[0], faces // out.shape[0]
    cb = a_lo.shape[0] - 2
    ca = b_lo.shape[0] - 1
    for k, halo in enumerate((a_lo, a_hi, b_lo, b_hi)):
        rows = cb if k < 2 else ca
        wide[k * rows * 8:(k + 1) * rows * 8] = (
            halo[0:rows, 0:8, :].astype(F32).reshape(rows * 8, width)
        )

    def edge(k, rows):
        return wide[pl.ds(k * rows * 8, rows, stride=8), :].astype(BF16)

    total[...] = base[...]
    total[0:cb] += dot(edge(0, cb), coupling[3])
    total[faces - cb:faces] += dot(edge(1, cb), coupling[4])
    total[pl.ds(0, ca, stride=cb), :] += dot(edge(2, ca), coupling[5])
    total[pl.ds(cb - 1, ca, stride=cb), :] += dot(edge(3, ca), coupling[6])
    picked = dot(pick[...], total[...].astype(BF16)).astype(BF16)
    here = lax.axis_index("gy")
    pb = a_lo.shape[1]
    top = a_lo[cb + 1].astype(F32)
    bottom = a_hi[cb].astype(F32)
    sub = lax.broadcasted_iota(jnp.int32, (MSG - slots, width), 0)

    def extra(o, column):
        rows = jnp.where(sub == 0, ids[o:o + 1, :], 0.0)
        rows = jnp.where(sub == 1, top[column:column + 1, :], rows)
        return jnp.where(sub == 2, bottom[column:column + 1, :], rows)

    for o in range(owners):
        out[o, 0:slots] = picked[o * slots:(o + 1) * slots]
        out[o, slots:MSG] = jnp.where(o > here, extra(o, pb - 1), extra(o, 0)).astype(BF16)


def update_body(adj, coupling, logf, a_lo, a_hi, b_lo, b_hi, after, out, prior, scale,
                held, field, once, sems):
    del after
    ca, cb, nl, width = adj.shape
    rows = cb * nl
    layer = lax.broadcasted_iota(jnp.int32, (rows, width), 0) % nl
    copies = []
    for a in range(ca):
        own = adj[a].reshape(rows, width)
        down = adj[a - 1] if a > 0 else a_lo[0:cb]
        up = adj[a + 1] if a < ca - 1 else a_hi[0:cb]
        total = dot(own, coupling[0])
        below = pltpu.roll(dot(own, coupling[1]), 1, 0)
        above = pltpu.roll(dot(own, coupling[2]), rows - 1, 0)
        total = total + jnp.where(layer > 0, below, 0.0) + jnp.where(layer < nl - 1, above, 0.0)
        total = total + dot(down.reshape(rows, width), coupling[3])
        total = total + dot(up.reshape(rows, width), coupling[4])
        before = jnp.concatenate([b_lo[a], own[:rows - nl]], axis=0)
        behind = jnp.concatenate([own[nl:], b_hi[a]], axis=0)
        total = total + dot(before, coupling[5]) + dot(behind, coupling[6])
        held[a] = total.astype(BF16).reshape(cb, nl, width)
        copy = pltpu.make_async_copy(held.at[a], out.at[a], sems.at[a])
        copy.start()
        copies.append(copy)
    pa, pb = logf.shape[0], logf.shape[1]
    off = 8
    field[...] = jnp.zeros(field.shape, F32)
    field[2:pa + 2, off:off + pb] = logf[...]
    field[0:2, off:off + pb] = a_lo[cb:cb + 2].astype(F32)
    field[pa + 2:pa + 4, off:off + pb] = a_hi[cb:cb + 2].astype(F32)
    side_lo, side_hi = b_lo[ca].astype(F32), b_hi[ca].astype(F32)
    for r in range(pa):
        for c in range(2):
            field[r + 2, off - 2 + c:off - 1 + c] = side_lo[c * pa + r:c * pa + r + 1]
            field[r + 2, off + pb + c:off + pb + c + 1] = side_hi[c * pa + r:c * pa + r + 1]

    def stencil(ref, a, b, na, nb):
        beside = ref[a + 1:a + 1 + na, b:b + nb] + ref[a - 1:a - 1 + na, b:b + nb]
        beside = beside + ref[a:a + na, b + 1:b + 1 + nb] + ref[a:a + na, b - 1:b - 1 + nb]
        return 1.3 * ref[a:a + na, b:b + nb] - 0.2 * beside

    i, j = lax.axis_index("gx"), lax.axis_index("gy")
    last_i, last_j = lax.axis_size("gx") - 1, lax.axis_size("gy") - 1
    once[...] = jnp.zeros(once.shape, F32)
    once[1:pa + 1, off:off + pb] = stencil(field, 2, off, pa, pb)
    once[0:1, off:off + pb] = jnp.where(i > 0, stencil(field, 1, off, 1, pb), 0.0)
    once[pa + 1:pa + 2, off:off + pb] = jnp.where(i < last_i, stencil(field, pa + 2, off, 1, pb), 0.0)
    once[1:pa + 1, off - 1:off] = jnp.where(j > 0, stencil(field, 2, off - 1, pa, 1), 0.0)
    once[1:pa + 1, off + pb:off + pb + 1] = jnp.where(j < last_j, stencil(field, 2, off + pb, pa, 1), 0.0)
    prior[...] = stencil(once, 1, off, pa, pb)
    scale[...] = jnp.exp(logf[...])
    for copy in copies:
        copy.wait()


def gradient_body(got, prior, scale, out):
    owners, _, width = got.shape
    pa, pb, _ = out.shape
    slots = 16
    per_row = width // slots
    tail = got[:, slots:MSG, :].astype(F32)
    listed = [jnp.sum(tail[k:k + per_row], axis=0)[0:1] for k in range(0, owners, per_row)]
    listed = jnp.concatenate(listed, axis=1)
    node = lax.broadcasted_iota(jnp.int32, (pa * pb, owners * slots), 0).astype(F32) + 1.0
    onehot = jnp.where(node == listed, 1.0, 0.0).astype(BF16)
    blocks = got[:, 0:slots, :].reshape(owners * slots, width)
    misfit = dot(onehot, blocks).reshape(pa, pb, width)
    out[...] = scale[...] * misfit + prior[...]
    j = lax.axis_index("gy")
    for side, column in ((-1, 0), (1, pb - 1)):
        inside = jnp.logical_and(j + side >= 0, j + side < owners)
        source = jnp.clip(j + side, 0, owners - 1)
        corners = jnp.where(inside, got[source, slots:MSG, :].astype(F32) * 0.08, 0.0)
        out[0, column:column + 1] += corners[1:2]
        out[pa - 1, column:column + 1] += corners[2:3]


def cost(flops, size):
    return pl.CostEstimate(flops=flops, bytes_accessed=size, transcendentals=0)


def per_device(adjoint_trace, coupling, log_friction, send_column, live_count, target_node):
    ca, cb, nl, width = adjoint_trace.shape
    pa, pb, _ = log_friction.shape
    owners = lax.axis_size("gy")
    faces = ca * cb
    shape = jax.ShapeDtypeStruct
    wire = pltpu.CompilerParams(vmem_limit_bytes=16 * 2**20)

    to_a_hi, to_a_lo, to_b_hi, to_b_lo = pl.pallas_call(
        pack_body,
        out_shape=(
            shape((cb + 2, nl, width), BF16),
            shape((cb + 2, nl, width), BF16),
            shape((ca + 1, nl, width), BF16),
            shape((ca + 1, nl, width), BF16),
        ),
        in_specs=[ANY, VMEM],
        out_specs=(VMEM,) * 4,
        scratch_shapes=[pltpu.SemaphoreType.DMA((4,))],
        compiler_params=wire,
        name="pack",
    )(adjoint_trace, log_friction)
    a_lo = shift(to_a_hi, "gx", 1)
    a_hi = shift(to_a_lo, "gx", -1)
    b_lo = shift(to_b_hi, "gy", 1)
    b_hi = shift(to_b_lo, "gy", -1)

    base, pick, ids = pl.pallas_call(
        local_body,
        out_shape=(
            shape((faces, width), F32),
            shape((faces, faces), BF16),
            shape((owners, width), F32),
        ),
        in_specs=[VMEM] * 5,
        out_specs=(VMEM,) * 3,
        scratch_shapes=[pltpu.VMEM((faces * 8, width), F32)],
        compiler_params=wire,
        cost_estimate=cost(2 * 6 * faces * width * width, 2 * 2**20),
        name="local",
    )(adjoint_trace, coupling, send_column, live_count, target_node)

    message = pl.pallas_call(
        message_body,
        out_shape=shape((owners, MSG, width), BF16),
        in_specs=[VMEM] * 8,
        out_specs=VMEM,
        scratch_shapes=[
            pltpu.VMEM((faces, width), F32),
            pltpu.VMEM((2 * (ca + cb) * 8, width), F32),
        ],
        compiler_params=wire,
        cost_estimate=cost(2 * faces * faces * width, 2**20),
        name="message",
    )(base, pick, ids, coupling, a_lo, a_hi, b_lo, b_hi)

    received = lax.all_to_all(message, "gy", split_axis=0, concat_axis=0, tiled=True)

    update, prior, scale = pl.pallas_call(
        update_body,
        out_shape=(
            shape(adjoint_trace.shape, BF16),
            shape(log_friction.shape, F32),
            shape(log_friction.shape, F32),
        ),
        in_specs=[VMEM] * 7 + [ANY],
        out_specs=(ANY, VMEM, VMEM),
        scratch_shapes=[
            pltpu.VMEM(adjoint_trace.shape, BF16),
            pltpu.VMEM((pa + 4, pb + 16, width), F32),
            pltpu.VMEM((pa + 2, pb + 16, width), F32),
            pltpu.SemaphoreType.DMA((ca,)),
        ],
        compiler_params=wire,
        cost_estimate=cost(2 * 7 * faces * nl * width * width, 4 * 2**20),
        name="update",
    )(adjoint_trace, coupling, log_friction, a_lo, a_hi, b_lo, b_hi, message)

    gradient = pl.pallas_call(
        gradient_body,
        out_shape=shape(log_friction.shape, F32),
        in_specs=[VMEM] * 3,
        out_specs=VMEM,
        compiler_params=wire,
        cost_estimate=cost(2 * pa * pb * faces * width, 2**19),
        name="gradient",
    )(received, prior, scale)
    return update, gradient


def solution(mesh):
    in_specs = (
        P("gx", "gy", None, None),
        P(),
        P("gx", "gy", None),
        P("gx", "gy", None),
        P("gx", "gy", None),
        P("gx", "gy", None, None),
    )
    out_specs = (P("gx", "gy", None, None), P("gx", "gy", None))
    return jax.shard_map(
        per_device, mesh=mesh, in_specs=in_specs, out_specs=out_specs, check_vma=False
    )
```

```python
import functools

import jax
import jax.numpy as jnp
from jax import lax
from jax.experimental import pallas as pl
from jax.experimental.pallas import tpu as pltpu
from jax.sharding import PartitionSpec as P

F32 = jnp.float32
BF16 = jnp.bfloat16
VMEM = pl.BlockSpec(memory_space=pltpu.VMEM)
ANY = pl.BlockSpec(memory_space=pl.ANY)
HBM = pl.BlockSpec(memory_space=pltpu.HBM)
MSG = 24


def dot(a, b):
    return jnp.dot(a, b, preferred_element_type=F32)


def in_hbm(array):
    return pltpu.with_memory_space_constraint(array, pltpu.HBM)


def shift(block, axis, step):
    count = lax.axis_size(axis)
    pairs = [(i, i + step) for i in range(count) if 0 <= i + step < count]
    return lax.ppermute(block, axis, pairs)


def pack_body(adj, logf_hbm, coupling, to_a_hi, to_a_lo, to_b_hi, to_b_lo, blocks, logf, sems):
    ca, cb = adj.shape[0], adj.shape[1]
    pa, pb = logf.shape[0], logf.shape[1]
    copies = [
        pltpu.make_async_copy(adj.at[ca - 1], to_a_hi.at[pl.ds(0, cb)], sems.at[0]),
        pltpu.make_async_copy(adj.at[0], to_a_lo.at[pl.ds(0, cb)], sems.at[1]),
        pltpu.make_async_copy(adj.at[:, cb - 1], to_b_hi.at[pl.ds(0, ca)], sems.at[2]),
        pltpu.make_async_copy(adj.at[:, 0], to_b_lo.at[pl.ds(0, ca)], sems.at[3]),
        pltpu.make_async_copy(coupling, blocks, sems.at[4]),
    ]
    fields = pltpu.make_async_copy(logf_hbm, logf, sems.at[5])
    fields.start()
    for copy in copies:
        copy.start()
    fields.wait()
    to_a_hi[cb:cb + 2] = logf[pa - 2:pa].astype(BF16)
    to_a_lo[cb:cb + 2] = logf[0:2].astype(BF16)
    to_b_hi[ca] = jnp.concatenate([logf[:, pb - 2, :], logf[:, pb - 1, :]], axis=0).astype(BF16)
    to_b_lo[ca] = jnp.concatenate([logf[:, 0, :], logf[:, 1, :]], axis=0).astype(BF16)
    for copy in copies:
        copy.wait()


def local_body(adj, coupling, send, live, nodes, base, pick, ids, wide):
    ca, cb, nl, width = adj.shape
    faces = ca * cb
    for a in range(ca):
        wide[a * cb * 8:(a + 1) * cb * 8] = adj[a, :, 0:8, :].astype(F32).reshape(cb * 8, width)
    low = wide[pl.ds(0, faces, stride=8), :].astype(BF16)
    above = wide[pl.ds(1, faces, stride=8), :].astype(BF16)
    total = dot(low, coupling[0]) + dot(above, coupling[2])
    zeros = jnp.zeros((cb, width), F32)
    total = total + jnp.concatenate([zeros, dot(low[:faces - cb], coupling[3])], axis=0)
    total = total + jnp.concatenate([dot(low[cb:], coupling[4]), zeros], axis=0)
    column = lax.broadcasted_iota(jnp.int32, (faces, width), 0) % cb
    before = pltpu.roll(dot(low, coupling[5]), 1, 0)
    after = pltpu.roll(dot(low, coupling[6]), faces - 1, 0)
    total = total + jnp.where(column > 0, before, 0.0) + jnp.where(column < cb - 1, after, 0.0)
    base[...] = total
    face = lax.broadcasted_iota(jnp.int32, (faces, faces), 0)
    picked_by = jnp.where(send[0] == face, 1.0, 0.0)
    pick[...] = picked_by.T.astype(BF16)
    owners, slots = nodes.shape[2], nodes.shape[3]
    sub = lax.broadcasted_iota(jnp.int32, (slots, width), 0)
    lane = lax.broadcasted_iota(jnp.int32, (slots, width), 1)
    spread = jnp.where(lane % slots == sub, 1.0, 0.0).astype(BF16)
    listed = dot(nodes[0, 0].astype(F32).astype(BF16), spread) + 1.0
    owner = lax.broadcasted_iota(jnp.int32, (owners, owners), 0)
    other = lax.broadcasted_iota(jnp.int32, (owners, owners), 1)
    counts = jnp.sum(jnp.where(owner == other, live[0].astype(F32), 0.0), axis=1, keepdims=True)
    lane = lax.broadcasted_iota(jnp.int32, (owners, width), 1)
    mine = lane // slots == lax.axis_index("gy") % (width // slots)
    alive = (lane % slots).astype(F32) < counts
    ids[...] = jnp.where(jnp.logical_and(mine, alive), listed, 0.0)


def message_body(base, pick, ids, coupling, a_lo, a_hi, b_lo, b_hi, out, total, wide):
    faces, width = base.shape
    owners, slots = out.shape[0], faces // out.shape[0]
    cb = a_lo.shape[0] - 2
    ca = b_lo.shape[0] - 1
    for k, halo in enumerate((a_lo, a_hi, b_lo, b_hi)):
        rows = cb if k < 2 else ca
        wide[k * rows * 8:(k + 1) * rows * 8] = (
            halo[0:rows, 0:8, :].astype(F32).reshape(rows * 8, width)
        )

    def edge(k, rows):
        return wide[pl.ds(k * rows * 8, rows, stride=8), :].astype(BF16)

    total[...] = base[...]
    total[0:cb] += dot(edge(0, cb), coupling[3])
    total[faces - cb:faces] += dot(edge(1, cb), coupling[4])
    total[pl.ds(0, ca, stride=cb), :] += dot(edge(2, ca), coupling[5])
    total[pl.ds(cb - 1, ca, stride=cb), :] += dot(edge(3, ca), coupling[6])
    picked = dot(pick[...], total[...].astype(BF16)).astype(BF16)
    here = lax.axis_index("gy")
    pb = a_lo.shape[1]
    top = a_lo[cb + 1].astype(F32)
    bottom = a_hi[cb].astype(F32)
    sub = lax.broadcasted_iota(jnp.int32, (MSG - slots, width), 0)

    def extra(o, column):
        rows = jnp.where(sub == 0, ids[o:o + 1, :], 0.0)
        rows = jnp.where(sub == 1, top[column:column + 1, :], rows)
        return jnp.where(sub == 2, bottom[column:column + 1, :], rows)

    for o in range(owners):
        out[o, 0:slots] = picked[o * slots:(o + 1) * slots]
        out[o, slots:MSG] = jnp.where(o > here, extra(o, pb - 1), extra(o, 0)).astype(BF16)


def update_body(adj, coupling, logf, a_lo, a_hi, b_lo, b_hi, out, prior, scale,
                held, field, once, sems):
    ca, cb, nl, width = adj.shape
    rows = cb * nl
    layer = lax.broadcasted_iota(jnp.int32, (rows, width), 0) % nl
    copies = []
    for a in range(ca):
        own = adj[a].reshape(rows, width)
        down = adj[a - 1] if a > 0 else a_lo[0:cb]
        up = adj[a + 1] if a < ca - 1 else a_hi[0:cb]
        total = dot(own, coupling[0])
        below = pltpu.roll(dot(own, coupling[1]), 1, 0)
        above = pltpu.roll(dot(own, coupling[2]), rows - 1, 0)
        total = total + jnp.where(layer > 0, below, 0.0) + jnp.where(layer < nl - 1, above, 0.0)
        total = total + dot(down.reshape(rows, width), coupling[3])
        total = total + dot(up.reshape(rows, width), coupling[4])
        before = jnp.concatenate([b_lo[a], own[:rows - nl]], axis=0)
        behind = jnp.concatenate([own[nl:], b_hi[a]], axis=0)
        total = total + dot(before, coupling[5]) + dot(behind, coupling[6])
        held[a] = total.astype(BF16).reshape(cb, nl, width)
        copy = pltpu.make_async_copy(held.at[a], out.at[a], sems.at[a])
        copy.start()
        copies.append(copy)
    pa, pb = logf.shape[0], logf.shape[1]
    off = 8
    field[...] = jnp.zeros(field.shape, F32)
    field[2:pa + 2, off:off + pb] = logf[...]
    field[0:2, off:off + pb] = a_lo[cb:cb + 2].astype(F32)
    field[pa + 2:pa + 4, off:off + pb] = a_hi[cb:cb + 2].astype(F32)
    side_lo, side_hi = b_lo[ca].astype(F32), b_hi[ca].astype(F32)
    for r in range(pa):
        for c in range(2):
            field[r + 2, off - 2 + c:off - 1 + c] = side_lo[c * pa + r:c * pa + r + 1]
            field[r + 2, off + pb + c:off + pb + c + 1] = side_hi[c * pa + r:c * pa + r + 1]

    def stencil(ref, a, b, na, nb):
        beside = ref[a + 1:a + 1 + na, b:b + nb] + ref[a - 1:a - 1 + na, b:b + nb]
        beside = beside + ref[a:a + na, b + 1:b + 1 + nb] + ref[a:a + na, b - 1:b - 1 + nb]
        return 1.3 * ref[a:a + na, b:b + nb] - 0.2 * beside

    i, j = lax.axis_index("gx"), lax.axis_index("gy")
    last_i, last_j = lax.axis_size("gx") - 1, lax.axis_size("gy") - 1
    once[...] = jnp.zeros(once.shape, F32)
    once[1:pa + 1, off:off + pb] = stencil(field, 2, off, pa, pb)
    once[0:1, off:off + pb] = jnp.where(i > 0, stencil(field, 1, off, 1, pb), 0.0)
    once[pa + 1:pa + 2, off:off + pb] = jnp.where(i < last_i, stencil(field, pa + 2, off, 1, pb), 0.0)
    once[1:pa + 1, off - 1:off] = jnp.where(j > 0, stencil(field, 2, off - 1, pa, 1), 0.0)
    once[1:pa + 1, off + pb:off + pb + 1] = jnp.where(j < last_j, stencil(field, 2, off + pb, pa, 1), 0.0)
    prior[...] = stencil(once, 1, off, pa, pb)
    scale[...] = jnp.exp(logf[...])
    for copy in copies:
        copy.wait()


def gradient_body(got, prior, scale, out):
    owners, _, width = got.shape
    pa, pb, _ = out.shape
    slots = 16
    per_row = width // slots
    tail = got[:, slots:MSG, :].astype(F32)
    listed = [jnp.sum(tail[k:k + per_row], axis=0)[0:1] for k in range(0, owners, per_row)]
    listed = jnp.concatenate(listed, axis=1)
    node = lax.broadcasted_iota(jnp.int32, (pa * pb, owners * slots), 0).astype(F32) + 1.0
    onehot = jnp.where(node == listed, 1.0, 0.0).astype(BF16)
    blocks = got[:, 0:slots, :].reshape(owners * slots, width)
    misfit = dot(onehot, blocks).reshape(pa, pb, width)
    out[...] = scale[...] * misfit + prior[...]
    j = lax.axis_index("gy")
    for side, column in ((-1, 0), (1, pb - 1)):
        inside = jnp.logical_and(j + side >= 0, j + side < owners)
        source = jnp.clip(j + side, 0, owners - 1)
        corners = jnp.where(inside, got[source, slots:MSG, :].astype(F32) * 0.08, 0.0)
        out[0, column:column + 1] += corners[1:2]
        out[pa - 1, column:column + 1] += corners[2:3]


def cost(flops, size):
    return pl.CostEstimate(flops=flops, bytes_accessed=size, transcendentals=0)


def per_device(adjoint_trace, coupling, log_friction, send_column, live_count, target_node):
    ca, cb, nl, width = adjoint_trace.shape
    pa, pb, _ = log_friction.shape
    owners = lax.axis_size("gy")
    faces = ca * cb
    shape = jax.ShapeDtypeStruct
    wire = pltpu.CompilerParams(vmem_limit_bytes=16 * 2**20)

    to_a_hi, to_a_lo, to_b_hi, to_b_lo, blocks = pl.pallas_call(
        pack_body,
        out_shape=(
            shape((cb + 2, nl, width), BF16),
            shape((cb + 2, nl, width), BF16),
            shape((ca + 1, nl, width), BF16),
            shape((ca + 1, nl, width), BF16),
            shape(coupling.shape, BF16),
        ),
        in_specs=[HBM] * 3,
        out_specs=(VMEM,) * 5,
        scratch_shapes=[pltpu.VMEM(log_friction.shape, F32), pltpu.SemaphoreType.DMA((6,))],
        compiler_params=wire,
        name="pack",
    )(in_hbm(adjoint_trace), in_hbm(log_friction), in_hbm(coupling))
    a_lo = shift(to_a_hi, "gx", 1)
    a_hi = shift(to_a_lo, "gx", -1)
    b_lo = shift(to_b_hi, "gy", 1)
    b_hi = shift(to_b_lo, "gy", -1)

    base, pick, ids = pl.pallas_call(
        local_body,
        out_shape=(
            shape((faces, width), F32),
            shape((faces, faces), BF16),
            shape((owners, width), F32),
        ),
        in_specs=[VMEM] * 5,
        out_specs=(VMEM,) * 3,
        scratch_shapes=[pltpu.VMEM((faces * 8, width), F32)],
        compiler_params=wire,
        cost_estimate=cost(2 * 6 * faces * width * width, 2 * 2**20),
        name="local",
    )(adjoint_trace, blocks, send_column, live_count, target_node)

    message = pl.pallas_call(
        message_body,
        out_shape=shape((owners, MSG, width), BF16),
        in_specs=[VMEM] * 8,
        out_specs=VMEM,
        scratch_shapes=[
            pltpu.VMEM((faces, width), F32),
            pltpu.VMEM((2 * (ca + cb) * 8, width), F32),
        ],
        compiler_params=wire,
        cost_estimate=cost(2 * faces * faces * width, 2**20),
        name="message",
    )(base, pick, ids, blocks, a_lo, a_hi, b_lo, b_hi)

    received = lax.all_to_all(message, "gy", split_axis=0, concat_axis=0, tiled=True)

    update, prior, scale = pl.pallas_call(
        update_body,
        out_shape=(
            shape(adjoint_trace.shape, BF16),
            shape(log_friction.shape, F32),
            shape(log_friction.shape, F32),
        ),
        in_specs=[VMEM] * 7,
        out_specs=(HBM, VMEM, VMEM),
        scratch_shapes=[
            pltpu.VMEM(adjoint_trace.shape, BF16),
            pltpu.VMEM((pa + 4, pb + 16, width), F32),
            pltpu.VMEM((pa + 2, pb + 16, width), F32),
            pltpu.SemaphoreType.DMA((ca,)),
        ],
        compiler_params=wire,
        cost_estimate=cost(2 * 7 * faces * nl * width * width, 4 * 2**20),
        name="update",
    )(adjoint_trace, blocks, log_friction, a_lo, a_hi, b_lo, b_hi)

    gradient = pl.pallas_call(
        gradient_body,
        out_shape=shape(log_friction.shape, F32),
        in_specs=[VMEM] * 3,
        out_specs=VMEM,
        compiler_params=wire,
        cost_estimate=cost(2 * pa * pb * faces * width, 2**19),
        name="gradient",
    )(received, prior, scale)
    return update, gradient


def solution(mesh):
    in_specs = (
        P("gx", "gy", None, None),
        P(),
        P("gx", "gy", None),
        P("gx", "gy", None),
        P("gx", "gy", None),
        P("gx", "gy", None, None),
    )
    out_specs = (P("gx", "gy", None, None), P("gx", "gy", None))
    return jax.shard_map(
        per_device, mesh=mesh, in_specs=in_specs, out_specs=out_specs, check_vma=False
    )
```

```python
import jax
import jax.numpy as jnp
from jax import lax
from jax.experimental import pallas as pl
from jax.experimental.pallas import tpu as pltpu
from jax.sharding import PartitionSpec as P

F32 = jnp.float32
BF16 = jnp.bfloat16
VMEM = pl.BlockSpec(memory_space=pltpu.VMEM)
HBM = pl.BlockSpec(memory_space=pltpu.HBM)
MSG = 24


def dot(a, b):
    return jnp.dot(a, b, preferred_element_type=F32)


def in_hbm(array):
    return pltpu.with_memory_space_constraint(array, pltpu.HBM)


def shift(block, axis, step):
    count = lax.axis_size(axis)
    pairs = [(i, i + step) for i in range(count) if 0 <= i + step < count]
    return lax.ppermute(block, axis, pairs)


def swap(block, first):
    count = lax.axis_size("gx")
    pairs = [(i, i + 1) for i in range(first, count - 1, 2)]
    return lax.ppermute(block, "gx", pairs + [(j, i) for i, j in pairs])


def pack_body(adj_hbm, logf_hbm, coupling_hbm, send_hbm, live_hbm, nodes_hbm,
              to_first, to_second, to_b_hi, to_b_lo, coupling, pick, ids,
              logf, send, live, nodes, sems):
    ca, cb = adj_hbm.shape[0], adj_hbm.shape[1]
    pa, pb, width = logf.shape
    odd = lax.axis_index("gx") % 2
    column = (ca - 1) * (1 - odd)
    row = (pa - 2) * (1 - odd)
    small = [
        pltpu.make_async_copy(source, target, sems.at[k])
        for k, (source, target) in enumerate(
            ((logf_hbm, logf), (send_hbm, send), (live_hbm, live), (nodes_hbm, nodes))
        )
    ]
    large = [
        pltpu.make_async_copy(source, target, sems.at[4 + k])
        for k, (source, target) in enumerate(
            (
                (adj_hbm.at[column], to_first.at[pl.ds(0, cb)]),
                (adj_hbm.at[ca - 1 - column], to_second.at[pl.ds(0, cb)]),
                (adj_hbm.at[:, cb - 1], to_b_hi.at[pl.ds(0, ca)]),
                (adj_hbm.at[:, 0], to_b_lo.at[pl.ds(0, ca)]),
                (coupling_hbm, coupling),
            )
        )
    ]
    for copy in small + large:
        copy.start()
    for copy in small:
        copy.wait()
    to_first[cb:cb + 2] = logf[pl.ds(row, 2)].astype(BF16)
    to_second[cb:cb + 2] = logf[pl.ds(pa - 2 - row, 2)].astype(BF16)
    to_b_hi[ca] = jnp.concatenate([logf[:, pb - 2, :], logf[:, pb - 1, :]], axis=0).astype(BF16)
    to_b_lo[ca] = jnp.concatenate([logf[:, 0, :], logf[:, 1, :]], axis=0).astype(BF16)
    faces = pick.shape[0]
    face = lax.broadcasted_iota(jnp.int32, (faces, faces), 0)
    pick[...] = jnp.where(send[0] == face, 1.0, 0.0).T.astype(BF16)
    owners, slots = nodes.shape[2], nodes.shape[3]
    sub = lax.broadcasted_iota(jnp.int32, (slots, width), 0)
    lane = lax.broadcasted_iota(jnp.int32, (slots, width), 1)
    spread = jnp.where(lane % slots == sub, 1.0, 0.0).astype(BF16)
    listed = dot(nodes[0, 0].astype(F32).astype(BF16), spread) + 1.0
    owner = lax.broadcasted_iota(jnp.int32, (owners, owners), 0)
    other = lax.broadcasted_iota(jnp.int32, (owners, owners), 1)
    counts = jnp.sum(jnp.where(owner == other, live[0].astype(F32), 0.0), axis=1, keepdims=True)
    lane = lax.broadcasted_iota(jnp.int32, (owners, width), 1)
    mine = lane // slots == lax.axis_index("gy") % (width // slots)
    alive = (lane % slots).astype(F32) < counts
    ids[...] = jnp.where(jnp.logical_and(mine, alive), listed, 0.0)
    for copy in large:
        copy.wait()


def local_body(adj, coupling, base, wide):
    ca, cb, nl, width = adj.shape
    faces = ca * cb
    for a in range(ca):
        wide[a * cb * 8:(a + 1) * cb * 8] = adj[a, :, 0:8, :].astype(F32).reshape(cb * 8, width)
    low = wide[pl.ds(0, faces, stride=8), :].astype(BF16)
    above = wide[pl.ds(1, faces, stride=8), :].astype(BF16)
    total = dot(low, coupling[0]) + dot(above, coupling[2])
    zeros = jnp.zeros((cb, width), F32)
    total = total + jnp.concatenate([zeros, dot(low[:faces - cb], coupling[3])], axis=0)
    total = total + jnp.concatenate([dot(low[cb:], coupling[4]), zeros], axis=0)
    column = lax.broadcasted_iota(jnp.int32, (faces, width), 0) % cb
    before = pltpu.roll(dot(low, coupling[5]), 1, 0)
    after = pltpu.roll(dot(low, coupling[6]), faces - 1, 0)
    total = total + jnp.where(column > 0, before, 0.0) + jnp.where(column < cb - 1, after, 0.0)
    base[...] = total


def message_body(base, pick, ids, coupling, first, second, b_lo, b_hi, out, total, wide):
    faces, width = base.shape
    owners, slots = out.shape[0], faces // out.shape[0]
    cb = first.shape[0] - 2
    ca = b_lo.shape[0] - 1
    odd = lax.axis_index("gx") % 2 == 1
    for k, halo in enumerate((first, second, b_lo, b_hi)):
        rows = cb if k < 2 else ca
        wide[k * rows * 8:(k + 1) * rows * 8] = (
            halo[0:rows, 0:8, :].astype(F32).reshape(rows * 8, width)
        )

    def row(k, rows):
        return wide[pl.ds(k * rows * 8, rows, stride=8), :]

    def edge(k, rows):
        if k < 2:
            return jnp.where(odd, row(k, rows), row(1 - k, rows)).astype(BF16)
        return row(k, rows).astype(BF16)

    total[...] = base[...]
    total[0:cb] += dot(edge(0, cb), coupling[3])
    total[faces - cb:faces] += dot(edge(1, cb), coupling[4])
    total[pl.ds(0, ca, stride=cb), :] += dot(edge(2, ca), coupling[5])
    total[pl.ds(cb - 1, ca, stride=cb), :] += dot(edge(3, ca), coupling[6])
    picked = dot(pick[...], total[...].astype(BF16)).astype(BF16)
    here = lax.axis_index("gy")
    pb = first.shape[1]
    top = jnp.where(odd, first[cb + 1].astype(F32), second[cb + 1].astype(F32))
    bottom = jnp.where(odd, second[cb].astype(F32), first[cb].astype(F32))
    sub = lax.broadcasted_iota(jnp.int32, (MSG - slots, width), 0)

    def extra(o, column):
        rows = jnp.where(sub == 0, ids[o:o + 1, :], 0.0)
        rows = jnp.where(sub == 1, top[column:column + 1, :], rows)
        return jnp.where(sub == 2, bottom[column:column + 1, :], rows)

    for o in range(owners):
        out[o, 0:slots] = picked[o * slots:(o + 1) * slots]
        out[o, slots:MSG] = jnp.where(o > here, extra(o, pb - 1), extra(o, 0)).astype(BF16)


def update_body(adj, coupling, logf, first, second, b_lo, b_hi, out, prior, scale,
                a_lo, a_hi, held, field, once, sems):
    ca, cb, nl, width = adj.shape
    rows = cb * nl
    layer = lax.broadcasted_iota(jnp.int32, (rows, width), 0) % nl
    odd = lax.axis_index("gx") % 2 == 1

    @pl.when(odd)
    def _():
        a_lo[...] = first[...]
        a_hi[...] = second[...]

    @pl.when(jnp.logical_not(odd))
    def _():
        a_lo[...] = second[...]
        a_hi[...] = first[...]

    copies = []
    for a in range(ca):
        own = adj[a].reshape(rows, width)
        down = adj[a - 1] if a > 0 else a_lo[0:cb]
        up = adj[a + 1] if a < ca - 1 else a_hi[0:cb]
        total = dot(own, coupling[0])
        below = pltpu.roll(dot(own, coupling[1]), 1, 0)
        above = pltpu.roll(dot(own, coupling[2]), rows - 1, 0)
        total = total + jnp.where(layer > 0, below, 0.0) + jnp.where(layer < nl - 1, above, 0.0)
        total = total + dot(down.reshape(rows, width), coupling[3])
        total = total + dot(up.reshape(rows, width), coupling[4])
        before = jnp.concatenate([b_lo[a], own[:rows - nl]], axis=0)
        behind = jnp.concatenate([own[nl:], b_hi[a]], axis=0)
        total = total + dot(before, coupling[5]) + dot(behind, coupling[6])
        held[a] = total.astype(BF16).reshape(cb, nl, width)
        copy = pltpu.make_async_copy(held.at[a], out.at[a], sems.at[a])
        copy.start()
        copies.append(copy)
    pa, pb = logf.shape[0], logf.shape[1]
    off = 8
    field[...] = jnp.zeros(field.shape, F32)
    field[2:pa + 2, off:off + pb] = logf[...]
    field[0:2, off:off + pb] = a_lo[cb:cb + 2].astype(F32)
    field[pa + 2:pa + 4, off:off + pb] = a_hi[cb:cb + 2].astype(F32)
    side_lo, side_hi = b_lo[ca].astype(F32), b_hi[ca].astype(F32)
    for r in range(pa):
        for c in range(2):
            field[r + 2, off - 2 + c:off - 1 + c] = side_lo[c * pa + r:c * pa + r + 1]
            field[r + 2, off + pb + c:off + pb + c + 1] = side_hi[c * pa + r:c * pa + r + 1]

    def stencil(ref, a, b, na, nb):
        beside = ref[a + 1:a + 1 + na, b:b + nb] + ref[a - 1:a - 1 + na, b:b + nb]
        beside = beside + ref[a:a + na, b + 1:b + 1 + nb] + ref[a:a + na, b - 1:b - 1 + nb]
        return 1.3 * ref[a:a + na, b:b + nb] - 0.2 * beside

    i, j = lax.axis_index("gx"), lax.axis_index("gy")
    last_i, last_j = lax.axis_size("gx") - 1, lax.axis_size("gy") - 1
    once[...] = jnp.zeros(once.shape, F32)
    once[1:pa + 1, off:off + pb] = stencil(field, 2, off, pa, pb)
    once[0:1, off:off + pb] = jnp.where(i > 0, stencil(field, 1, off, 1, pb), 0.0)
    once[pa + 1:pa + 2, off:off + pb] = jnp.where(i < last_i, stencil(field, pa + 2, off, 1, pb), 0.0)
    once[1:pa + 1, off - 1:off] = jnp.where(j > 0, stencil(field, 2, off - 1, pa, 1), 0.0)
    once[1:pa + 1, off + pb:off + pb + 1] = jnp.where(j < last_j, stencil(field, 2, off + pb, pa, 1), 0.0)
    prior[...] = stencil(once, 1, off, pa, pb)
    scale[...] = jnp.exp(logf[...])
    for copy in copies:
        copy.wait()


def gradient_body(got, prior, scale, out):
    owners, _, width = got.shape
    pa, pb, _ = out.shape
    slots = 16
    per_row = width // slots
    tail = got[:, slots:MSG, :].astype(F32)
    listed = [jnp.sum(tail[k:k + per_row], axis=0)[0:1] for k in range(0, owners, per_row)]
    listed = jnp.concatenate(listed, axis=1)
    node = lax.broadcasted_iota(jnp.int32, (pa * pb, owners * slots), 0).astype(F32) + 1.0
    onehot = jnp.where(node == listed, 1.0, 0.0).astype(BF16)
    blocks = got[:, 0:slots, :].reshape(owners * slots, width)
    misfit = dot(onehot, blocks).reshape(pa, pb, width)
    out[...] = scale[...] * misfit + prior[...]
    j = lax.axis_index("gy")
    for side, column in ((-1, 0), (1, pb - 1)):
        inside = jnp.logical_and(j + side >= 0, j + side < owners)
        source = jnp.clip(j + side, 0, owners - 1)
        corners = jnp.where(inside, got[source, slots:MSG, :].astype(F32) * 0.08, 0.0)
        out[0, column:column + 1] += corners[1:2]
        out[pa - 1, column:column + 1] += corners[2:3]


def cost(flops, size):
    return pl.CostEstimate(flops=flops, bytes_accessed=size, transcendentals=0)


def per_device(adjoint_trace, coupling, log_friction, send_column, live_count, target_node):
    ca, cb, nl, width = adjoint_trace.shape
    pa, pb, _ = log_friction.shape
    owners = lax.axis_size("gy")
    faces = ca * cb
    shape = jax.ShapeDtypeStruct
    wire = pltpu.CompilerParams(vmem_limit_bytes=16 * 2**20)

    to_first, to_second, to_b_hi, to_b_lo, blocks, pick, ids = pl.pallas_call(
        pack_body,
        out_shape=(
            shape((cb + 2, nl, width), BF16),
            shape((cb + 2, nl, width), BF16),
            shape((ca + 1, nl, width), BF16),
            shape((ca + 1, nl, width), BF16),
            shape(coupling.shape, BF16),
            shape((faces, faces), BF16),
            shape((owners, width), F32),
        ),
        in_specs=[HBM] * 6,
        out_specs=(VMEM,) * 7,
        scratch_shapes=[
            pltpu.VMEM(log_friction.shape, F32),
            pltpu.VMEM(send_column.shape, jnp.int32),
            pltpu.VMEM(live_count.shape, jnp.int32),
            pltpu.VMEM(target_node.shape, jnp.int32),
            pltpu.SemaphoreType.DMA((9,)),
        ],
        compiler_params=wire,
        name="pack",
    )(*map(in_hbm, (adjoint_trace, log_friction, coupling, send_column, live_count, target_node)))
    first = swap(to_first, 0)
    second = swap(to_second, 1)
    b_lo = shift(to_b_hi, "gy", 1)
    b_hi = shift(to_b_lo, "gy", -1)

    base = pl.pallas_call(
        local_body,
        out_shape=shape((faces, width), F32),
        in_specs=[VMEM] * 2,
        out_specs=VMEM,
        scratch_shapes=[pltpu.VMEM((faces * 8, width), F32)],
        compiler_params=wire,
        cost_estimate=cost(2 * 6 * faces * width * width, 2 * 2**20),
        name="local",
    )(adjoint_trace, blocks)

    message = pl.pallas_call(
        message_body,
        out_shape=shape((owners, MSG, width), BF16),
        in_specs=[VMEM] * 8,
        out_specs=VMEM,
        scratch_shapes=[
            pltpu.VMEM((faces, width), F32),
            pltpu.VMEM((2 * (ca + cb) * 8, width), F32),
        ],
        compiler_params=wire,
        cost_estimate=cost(2 * faces * faces * width, 2**20),
        name="message",
    )(base, pick, ids, blocks, first, second, b_lo, b_hi)

    received = lax.all_to_all(message, "gy", split_axis=0, concat_axis=0, tiled=True)

    update, prior, scale = pl.pallas_call(
        update_body,
        out_shape=(
            shape(adjoint_trace.shape, BF16),
            shape(log_friction.shape, F32),
            shape(log_friction.shape, F32),
        ),
        in_specs=[VMEM] * 7,
        out_specs=(HBM, VMEM, VMEM),
        scratch_shapes=[
            pltpu.VMEM((cb + 2, nl, width), BF16),
            pltpu.VMEM((cb + 2, nl, width), BF16),
            pltpu.VMEM(adjoint_trace.shape, BF16),
            pltpu.VMEM((pa + 4, pb + 16, width), F32),
            pltpu.VMEM((pa + 2, pb + 16, width), F32),
            pltpu.SemaphoreType.DMA((ca,)),
        ],
        compiler_params=wire,
        cost_estimate=cost(2 * 7 * faces * nl * width * width, 4 * 2**20),
        name="update",
    )(adjoint_trace, blocks, log_friction, first, second, b_lo, b_hi)

    gradient = pl.pallas_call(
        gradient_body,
        out_shape=shape(log_friction.shape, F32),
        in_specs=[VMEM] * 3,
        out_specs=VMEM,
        compiler_params=wire,
        cost_estimate=cost(2 * pa * pb * faces * width, 2**19),
        name="gradient",
    )(received, prior, scale)
    return update, gradient


def solution(mesh):
    in_specs = (
        P("gx", "gy", None, None),
        P(),
        P("gx", "gy", None),
        P("gx", "gy", None),
        P("gx", "gy", None),
        P("gx", "gy", None, None),
    )
    out_specs = (P("gx", "gy", None, None), P("gx", "gy", None))
    return jax.shard_map(
        per_device, mesh=mesh, in_specs=in_specs, out_specs=out_specs, check_vma=False
    )
```

```python
import jax
import jax.numpy as jnp
from jax import lax
from jax.experimental import pallas as pl
from jax.experimental.pallas import tpu as pltpu
from jax.sharding import PartitionSpec as P

F32 = jnp.float32
BF16 = jnp.bfloat16
VMEM = pl.BlockSpec(memory_space=pltpu.VMEM)
HBM = pl.BlockSpec(memory_space=pltpu.HBM)
MSG = 24


def dot(a, b):
    return jnp.dot(a, b, preferred_element_type=F32)


def in_hbm(array):
    return pltpu.with_memory_space_constraint(array, pltpu.HBM)


def shift(block, axis, step):
    count = lax.axis_size(axis)
    pairs = [(i, i + step) for i in range(count) if 0 <= i + step < count]
    return lax.ppermute(block, axis, pairs)


def swap(block, first):
    count = lax.axis_size("gy")
    pairs = [(i, i + 1) for i in range(first, count - 1, 2)]
    return lax.ppermute(block, "gy", pairs + [(j, i) for i, j in pairs])


def pack_body(adj_hbm, logf_hbm, coupling_hbm, to_a_hi, to_a_lo, to_far, to_near, coupling,
              logf, sems):
    ca, cb = adj_hbm.shape[0], adj_hbm.shape[1]
    pa, pb, _ = logf.shape
    odd = lax.axis_index("gy") % 2
    column = (cb - 1) * (1 - odd)
    fields = pltpu.make_async_copy(logf_hbm, logf, sems.at[0])
    copies = [
        pltpu.make_async_copy(source, target, sems.at[1 + k])
        for k, (source, target) in enumerate(
            (
                (adj_hbm.at[ca - 1], to_a_hi.at[pl.ds(0, cb)]),
                (adj_hbm.at[0], to_a_lo.at[pl.ds(0, cb)]),
                (adj_hbm.at[:, cb - 1 - column], to_far.at[pl.ds(0, ca)]),
                (adj_hbm.at[:, column], to_near.at[pl.ds(0, ca)]),
                (coupling_hbm, coupling),
            )
        )
    ]
    fields.start()
    for copy in copies:
        copy.start()
    fields.wait()
    to_a_hi[cb:cb + 2] = logf[pa - 2:pa].astype(BF16)
    to_a_lo[cb:cb + 2] = logf[0:2].astype(BF16)
    hi = jnp.concatenate([logf[:, pb - 2, :], logf[:, pb - 1, :]], axis=0)
    lo = jnp.concatenate([logf[:, 0, :], logf[:, 1, :]], axis=0)
    to_far[ca] = jnp.where(odd == 1, hi, lo).astype(BF16)
    to_near[ca] = jnp.where(odd == 1, lo, hi).astype(BF16)
    for copy in copies:
        copy.wait()


def local_body(adj, coupling, send, live, nodes, base, pick, ids, wide):
    ca, cb, nl, width = adj.shape
    faces = ca * cb
    for a in range(ca):
        wide[a * cb * 8:(a + 1) * cb * 8] = adj[a, :, 0:8, :].astype(F32).reshape(cb * 8, width)
    low = wide[pl.ds(0, faces, stride=8), :].astype(BF16)
    above = wide[pl.ds(1, faces, stride=8), :].astype(BF16)
    total = dot(low, coupling[0]) + dot(above, coupling[2])
    zeros = jnp.zeros((cb, width), F32)
    total = total + jnp.concatenate([zeros, dot(low[:faces - cb], coupling[3])], axis=0)
    total = total + jnp.concatenate([dot(low[cb:], coupling[4]), zeros], axis=0)
    column = lax.broadcasted_iota(jnp.int32, (faces, width), 0) % cb
    before = pltpu.roll(dot(low, coupling[5]), 1, 0)
    after = pltpu.roll(dot(low, coupling[6]), faces - 1, 0)
    total = total + jnp.where(column > 0, before, 0.0) + jnp.where(column < cb - 1, after, 0.0)
    base[...] = total
    face = lax.broadcasted_iota(jnp.int32, (faces, faces), 0)
    pick[...] = jnp.where(send[0] == face, 1.0, 0.0).T.astype(BF16)
    owners, slots = nodes.shape[2], nodes.shape[3]
    sub = lax.broadcasted_iota(jnp.int32, (slots, width), 0)
    lane = lax.broadcasted_iota(jnp.int32, (slots, width), 1)
    spread = jnp.where(lane % slots == sub, 1.0, 0.0).astype(BF16)
    listed = dot(nodes[0, 0].astype(F32).astype(BF16), spread) + 1.0
    owner = lax.broadcasted_iota(jnp.int32, (owners, owners), 0)
    other = lax.broadcasted_iota(jnp.int32, (owners, owners), 1)
    counts = jnp.sum(jnp.where(owner == other, live[0].astype(F32), 0.0), axis=1, keepdims=True)
    lane = lax.broadcasted_iota(jnp.int32, (owners, width), 1)
    mine = lane // slots == lax.axis_index("gy") % (width // slots)
    alive = (lane % slots).astype(F32) < counts
    ids[...] = jnp.where(jnp.logical_and(mine, alive), listed, 0.0)


def message_body(base, pick, ids, coupling, a_lo, a_hi, far, near, out, total, wide):
    faces, width = base.shape
    owners, slots = out.shape[0], faces // out.shape[0]
    cb = a_lo.shape[0] - 2
    ca = far.shape[0] - 1
    here = lax.axis_index("gy")
    odd = here % 2 == 1
    for k, halo in enumerate((a_lo, a_hi, far, near)):
        rows = cb if k < 2 else ca
        wide[k * rows * 8:(k + 1) * rows * 8] = (
            halo[0:rows, 0:8, :].astype(F32).reshape(rows * 8, width)
        )

    def row(k, rows):
        return wide[pl.ds(k * rows * 8, rows, stride=8), :]

    def edge(k, rows):
        if k < 2:
            return row(k, rows).astype(BF16)
        return jnp.where(odd, row(5 - k, rows), row(k, rows)).astype(BF16)

    total[...] = base[...]
    total[0:cb] += dot(edge(0, cb), coupling[3])
    total[faces - cb:faces] += dot(edge(1, cb), coupling[4])
    total[pl.ds(0, ca, stride=cb), :] += dot(edge(2, ca), coupling[5])
    total[pl.ds(cb - 1, ca, stride=cb), :] += dot(edge(3, ca), coupling[6])
    picked = dot(pick[...], total[...].astype(BF16)).astype(BF16)
    pb = a_lo.shape[1]
    top = a_lo[cb + 1].astype(F32)
    bottom = a_hi[cb].astype(F32)
    sub = lax.broadcasted_iota(jnp.int32, (MSG - slots, width), 0)

    def extra(o, column):
        rows = jnp.where(sub == 0, ids[o:o + 1, :], 0.0)
        rows = jnp.where(sub == 1, top[column:column + 1, :], rows)
        return jnp.where(sub == 2, bottom[column:column + 1, :], rows)

    for o in range(owners):
        out[o, 0:slots] = picked[o * slots:(o + 1) * slots]
        out[o, slots:MSG] = jnp.where(o > here, extra(o, pb - 1), extra(o, 0)).astype(BF16)


def update_body(adj, coupling, logf, a_lo, a_hi, far, near, out, prior, scale,
                b_lo, b_hi, held, field, once, sems):
    ca, cb, nl, width = adj.shape
    rows = cb * nl
    layer = lax.broadcasted_iota(jnp.int32, (rows, width), 0) % nl
    odd = lax.axis_index("gy") % 2 == 1

    @pl.when(odd)
    def _():
        b_lo[...] = near[...]
        b_hi[...] = far[...]

    @pl.when(jnp.logical_not(odd))
    def _():
        b_lo[...] = far[...]
        b_hi[...] = near[...]

    copies = []
    for a in range(ca):
        own = adj[a].reshape(rows, width)
        down = adj[a - 1] if a > 0 else a_lo[0:cb]
        up = adj[a + 1] if a < ca - 1 else a_hi[0:cb]
        total = dot(own, coupling[0])
        below = pltpu.roll(dot(own, coupling[1]), 1, 0)
        above = pltpu.roll(dot(own, coupling[2]), rows - 1, 0)
        total = total + jnp.where(layer > 0, below, 0.0) + jnp.where(layer < nl - 1, above, 0.0)
        total = total + dot(down.reshape(rows, width), coupling[3])
        total = total + dot(up.reshape(rows, width), coupling[4])
        before = jnp.concatenate([b_lo[a], own[:rows - nl]], axis=0)
        behind = jnp.concatenate([own[nl:], b_hi[a]], axis=0)
        total = total + dot(before, coupling[5]) + dot(behind, coupling[6])
        held[a] = total.astype(BF16).reshape(cb, nl, width)
        copy = pltpu.make_async_copy(held.at[a], out.at[a], sems.at[a])
        copy.start()
        copies.append(copy)
    pa, pb = logf.shape[0], logf.shape[1]
    off = 8
    field[...] = jnp.zeros(field.shape, F32)
    field[2:pa + 2, off:off + pb] = logf[...]
    field[0:2, off:off + pb] = a_lo[cb:cb + 2].astype(F32)
    field[pa + 2:pa + 4, off:off + pb] = a_hi[cb:cb + 2].astype(F32)
    side_lo, side_hi = b_lo[ca].astype(F32), b_hi[ca].astype(F32)
    for r in range(pa):
        for c in range(2):
            field[r + 2, off - 2 + c:off - 1 + c] = side_lo[c * pa + r:c * pa + r + 1]
            field[r + 2, off + pb + c:off + pb + c + 1] = side_hi[c * pa + r:c * pa + r + 1]

    def stencil(ref, a, b, na, nb):
        beside = ref[a + 1:a + 1 + na, b:b + nb] + ref[a - 1:a - 1 + na, b:b + nb]
        beside = beside + ref[a:a + na, b + 1:b + 1 + nb] + ref[a:a + na, b - 1:b - 1 + nb]
        return 1.3 * ref[a:a + na, b:b + nb] - 0.2 * beside

    i, j = lax.axis_index("gx"), lax.axis_index("gy")
    last_i, last_j = lax.axis_size("gx") - 1, lax.axis_size("gy") - 1
    once[...] = jnp.zeros(once.shape, F32)
    once[1:pa + 1, off:off + pb] = stencil(field, 2, off, pa, pb)
    once[0:1, off:off + pb] = jnp.where(i > 0, stencil(field, 1, off, 1, pb), 0.0)
    once[pa + 1:pa + 2, off:off + pb] = jnp.where(i < last_i, stencil(field, pa + 2, off, 1, pb), 0.0)
    once[1:pa + 1, off - 1:off] = jnp.where(j > 0, stencil(field, 2, off - 1, pa, 1), 0.0)
    once[1:pa + 1, off + pb:off + pb + 1] = jnp.where(j < last_j, stencil(field, 2, off + pb, pa, 1), 0.0)
    prior[...] = stencil(once, 1, off, pa, pb)
    scale[...] = jnp.exp(logf[...])
    for copy in copies:
        copy.wait()


def gradient_body(got, prior, scale, out):
    owners, _, width = got.shape
    pa, pb, _ = out.shape
    slots = 16
    per_row = width // slots
    tail = got[:, slots:MSG, :].astype(F32)
    listed = [jnp.sum(tail[k:k + per_row], axis=0)[0:1] for k in range(0, owners, per_row)]
    listed = jnp.concatenate(listed, axis=1)
    node = lax.broadcasted_iota(jnp.int32, (pa * pb, owners * slots), 0).astype(F32) + 1.0
    onehot = jnp.where(node == listed, 1.0, 0.0).astype(BF16)
    blocks = got[:, 0:slots, :].reshape(owners * slots, width)
    misfit = dot(onehot, blocks).reshape(pa, pb, width)
    out[...] = scale[...] * misfit + prior[...]
    j = lax.axis_index("gy")
    for side, column in ((-1, 0), (1, pb - 1)):
        inside = jnp.logical_and(j + side >= 0, j + side < owners)
        source = jnp.clip(j + side, 0, owners - 1)
        corners = jnp.where(inside, got[source, slots:MSG, :].astype(F32) * 0.08, 0.0)
        out[0, column:column + 1] += corners[1:2]
        out[pa - 1, column:column + 1] += corners[2:3]


def cost(flops, size):
    return pl.CostEstimate(flops=flops, bytes_accessed=size, transcendentals=0)


def per_device(adjoint_trace, coupling, log_friction, send_column, live_count, target_node):
    ca, cb, nl, width = adjoint_trace.shape
    pa, pb, _ = log_friction.shape
    owners = lax.axis_size("gy")
    faces = ca * cb
    shape = jax.ShapeDtypeStruct
    wire = pltpu.CompilerParams(vmem_limit_bytes=16 * 2**20)

    to_a_hi, to_a_lo, to_far, to_near, blocks = pl.pallas_call(
        pack_body,
        out_shape=(
            shape((cb + 2, nl, width), BF16),
            shape((cb + 2, nl, width), BF16),
            shape((ca + 1, nl, width), BF16),
            shape((ca + 1, nl, width), BF16),
            shape(coupling.shape, BF16),
        ),
        in_specs=[HBM] * 3,
        out_specs=(VMEM,) * 5,
        scratch_shapes=[pltpu.VMEM(log_friction.shape, F32), pltpu.SemaphoreType.DMA((6,))],
        compiler_params=wire,
        name="pack",
    )(*map(in_hbm, (adjoint_trace, log_friction, coupling)))
    a_lo = shift(to_a_hi, "gx", 1)
    a_hi = shift(to_a_lo, "gx", -1)
    far = swap(to_far, 1)
    near = swap(to_near, 0)

    base, pick, ids = pl.pallas_call(
        local_body,
        out_shape=(
            shape((faces, width), F32),
            shape((faces, faces), BF16),
            shape((owners, width), F32),
        ),
        in_specs=[VMEM] * 5,
        out_specs=(VMEM,) * 3,
        scratch_shapes=[pltpu.VMEM((faces * 8, width), F32)],
        compiler_params=wire,
        cost_estimate=cost(2 * 6 * faces * width * width, 2 * 2**20),
        name="local",
    )(adjoint_trace, blocks, send_column, live_count, target_node)

    message = pl.pallas_call(
        message_body,
        out_shape=shape((owners, MSG, width), BF16),
        in_specs=[VMEM] * 8,
        out_specs=VMEM,
        scratch_shapes=[
            pltpu.VMEM((faces, width), F32),
            pltpu.VMEM((2 * (ca + cb) * 8, width), F32),
        ],
        compiler_params=wire,
        cost_estimate=cost(2 * faces * faces * width, 2**20),
        name="message",
    )(base, pick, ids, blocks, a_lo, a_hi, far, near)

    received = lax.all_to_all(message, "gy", split_axis=0, concat_axis=0, tiled=True)

    update, prior, scale = pl.pallas_call(
        update_body,
        out_shape=(
            shape(adjoint_trace.shape, BF16),
            shape(log_friction.shape, F32),
            shape(log_friction.shape, F32),
        ),
        in_specs=[VMEM] * 7,
        out_specs=(HBM, VMEM, VMEM),
        scratch_shapes=[
            pltpu.VMEM((ca + 1, nl, width), BF16),
            pltpu.VMEM((ca + 1, nl, width), BF16),
            pltpu.VMEM(adjoint_trace.shape, BF16),
            pltpu.VMEM((pa + 4, pb + 16, width), F32),
            pltpu.VMEM((pa + 2, pb + 16, width), F32),
            pltpu.SemaphoreType.DMA((ca,)),
        ],
        compiler_params=wire,
        cost_estimate=cost(2 * 7 * faces * nl * width * width, 4 * 2**20),
        name="update",
    )(adjoint_trace, blocks, log_friction, a_lo, a_hi, far, near)

    gradient = pl.pallas_call(
        gradient_body,
        out_shape=shape(log_friction.shape, F32),
        in_specs=[VMEM] * 3,
        out_specs=VMEM,
        compiler_params=wire,
        cost_estimate=cost(2 * pa * pb * faces * width, 2**19),
        name="gradient",
    )(received, prior, scale)
    return update, gradient


def solution(mesh):
    in_specs = (
        P("gx", "gy", None, None),
        P(),
        P("gx", "gy", None),
        P("gx", "gy", None),
        P("gx", "gy", None),
        P("gx", "gy", None, None),
    )
    out_specs = (P("gx", "gy", None, None), P("gx", "gy", None))
    return jax.shard_map(
        per_device, mesh=mesh, in_specs=in_specs, out_specs=out_specs, check_vma=False
    )
```

```python
import jax
import jax.numpy as jnp
from jax import lax
from jax.experimental import pallas as pl
from jax.experimental.pallas import tpu as pltpu
from jax.sharding import PartitionSpec as P

F32 = jnp.float32
BF16 = jnp.bfloat16
VMEM = pl.BlockSpec(memory_space=pltpu.VMEM)
HBM = pl.BlockSpec(memory_space=pltpu.HBM)
MSG = 24


def dot(a, b):
    return jnp.dot(a, b, preferred_element_type=F32)


def in_hbm(array):
    return pltpu.with_memory_space_constraint(array, pltpu.HBM)


def swap(block, axis, first):
    count = lax.axis_size(axis)
    pairs = [(i, i + 1) for i in range(first, count - 1, 2)]
    return lax.ppermute(block, axis, pairs + [(j, i) for i, j in pairs])


def pack_body(adj_hbm, logf_hbm, coupling_hbm, to_a_far, to_a_near, to_b_far, to_b_near, coupling,
              logf, sems):
    ca, cb = adj_hbm.shape[0], adj_hbm.shape[1]
    pa, pb, _ = logf.shape
    odd_a, odd_b = lax.axis_index("gx") % 2, lax.axis_index("gy") % 2
    near_a, near_b = (ca - 1) * (1 - odd_a), (cb - 1) * (1 - odd_b)
    row = (pa - 2) * (1 - odd_a)
    fields = pltpu.make_async_copy(logf_hbm, logf, sems.at[0])
    copies = [
        pltpu.make_async_copy(source, target, sems.at[1 + k])
        for k, (source, target) in enumerate(
            (
                (adj_hbm.at[ca - 1 - near_a], to_a_far.at[pl.ds(0, cb)]),
                (adj_hbm.at[near_a], to_a_near.at[pl.ds(0, cb)]),
                (adj_hbm.at[:, cb - 1 - near_b], to_b_far.at[pl.ds(0, ca)]),
                (adj_hbm.at[:, near_b], to_b_near.at[pl.ds(0, ca)]),
                (coupling_hbm, coupling),
            )
        )
    ]
    fields.start()
    for copy in copies:
        copy.start()
    fields.wait()
    to_a_far[cb:cb + 2] = logf[pl.ds(pa - 2 - row, 2)].astype(BF16)
    to_a_near[cb:cb + 2] = logf[pl.ds(row, 2)].astype(BF16)
    hi = jnp.concatenate([logf[:, pb - 2, :], logf[:, pb - 1, :]], axis=0)
    lo = jnp.concatenate([logf[:, 0, :], logf[:, 1, :]], axis=0)
    to_b_far[ca] = jnp.where(odd_b == 1, hi, lo).astype(BF16)
    to_b_near[ca] = jnp.where(odd_b == 1, lo, hi).astype(BF16)
    for copy in copies:
        copy.wait()


def local_body(adj, coupling, send, live, nodes, base, pick, ids, wide):
    ca, cb, nl, width = adj.shape
    faces = ca * cb
    for a in range(ca):
        wide[a * cb * 8:(a + 1) * cb * 8] = adj[a, :, 0:8, :].astype(F32).reshape(cb * 8, width)
    low = wide[pl.ds(0, faces, stride=8), :].astype(BF16)
    above = wide[pl.ds(1, faces, stride=8), :].astype(BF16)
    total = dot(low, coupling[0]) + dot(above, coupling[2])
    zeros = jnp.zeros((cb, width), F32)
    total = total + jnp.concatenate([zeros, dot(low[:faces - cb], coupling[3])], axis=0)
    total = total + jnp.concatenate([dot(low[cb:], coupling[4]), zeros], axis=0)
    column = lax.broadcasted_iota(jnp.int32, (faces, width), 0) % cb
    before = pltpu.roll(dot(low, coupling[5]), 1, 0)
    after = pltpu.roll(dot(low, coupling[6]), faces - 1, 0)
    total = total + jnp.where(column > 0, before, 0.0) + jnp.where(column < cb - 1, after, 0.0)
    base[...] = total
    face = lax.broadcasted_iota(jnp.int32, (faces, faces), 0)
    pick[...] = jnp.where(send[0] == face, 1.0, 0.0).T.astype(BF16)
    owners, slots = nodes.shape[2], nodes.shape[3]
    sub = lax.broadcasted_iota(jnp.int32, (slots, width), 0)
    lane = lax.broadcasted_iota(jnp.int32, (slots, width), 1)
    spread = jnp.where(lane % slots == sub, 1.0, 0.0).astype(BF16)
    listed = dot(nodes[0, 0].astype(F32).astype(BF16), spread) + 1.0
    owner = lax.broadcasted_iota(jnp.int32, (owners, owners), 0)
    other = lax.broadcasted_iota(jnp.int32, (owners, owners), 1)
    counts = jnp.sum(jnp.where(owner == other, live[0].astype(F32), 0.0), axis=1, keepdims=True)
    lane = lax.broadcasted_iota(jnp.int32, (owners, width), 1)
    mine = lane // slots == lax.axis_index("gy") % (width // slots)
    alive = (lane % slots).astype(F32) < counts
    ids[...] = jnp.where(jnp.logical_and(mine, alive), listed, 0.0)


def message_body(base, pick, ids, coupling, a_far, a_near, b_far, b_near, out, total, wide):
    faces, width = base.shape
    owners, slots = out.shape[0], faces // out.shape[0]
    cb = a_far.shape[0] - 2
    ca = b_far.shape[0] - 1
    here = lax.axis_index("gy")
    odd_a, odd_b = lax.axis_index("gx") % 2 == 1, here % 2 == 1
    for k, halo in enumerate((a_far, a_near, b_far, b_near)):
        rows = cb if k < 2 else ca
        wide[k * rows * 8:(k + 1) * rows * 8] = (
            halo[0:rows, 0:8, :].astype(F32).reshape(rows * 8, width)
        )

    def row(k, rows):
        return wide[pl.ds(k * rows * 8, rows, stride=8), :]

    def edge(k, rows):
        odd = odd_a if k < 2 else odd_b
        return jnp.where(odd, row(k ^ 1, rows), row(k, rows)).astype(BF16)

    total[...] = base[...]
    total[0:cb] += dot(edge(0, cb), coupling[3])
    total[faces - cb:faces] += dot(edge(1, cb), coupling[4])
    total[pl.ds(0, ca, stride=cb), :] += dot(edge(2, ca), coupling[5])
    total[pl.ds(cb - 1, ca, stride=cb), :] += dot(edge(3, ca), coupling[6])
    picked = dot(pick[...], total[...].astype(BF16)).astype(BF16)
    pb = a_far.shape[1]
    top = jnp.where(odd_a, a_near[cb + 1].astype(F32), a_far[cb + 1].astype(F32))
    bottom = jnp.where(odd_a, a_far[cb].astype(F32), a_near[cb].astype(F32))
    sub = lax.broadcasted_iota(jnp.int32, (MSG - slots, width), 0)

    def extra(o, column):
        rows = jnp.where(sub == 0, ids[o:o + 1, :], 0.0)
        rows = jnp.where(sub == 1, top[column:column + 1, :], rows)
        return jnp.where(sub == 2, bottom[column:column + 1, :], rows)

    for o in range(owners):
        out[o, 0:slots] = picked[o * slots:(o + 1) * slots]
        out[o, slots:MSG] = jnp.where(o > here, extra(o, pb - 1), extra(o, 0)).astype(BF16)


def update_body(adj, coupling, logf, a_far, a_near, b_far, b_near, out, prior, scale,
                a_lo, a_hi, b_lo, b_hi, held, field, once, sems):
    ca, cb, nl, width = adj.shape
    rows = cb * nl
    layer = lax.broadcasted_iota(jnp.int32, (rows, width), 0) % nl
    for axis, far, near, lo, hi in (
        ("gx", a_far, a_near, a_lo, a_hi), ("gy", b_far, b_near, b_lo, b_hi)
    ):
        odd = lax.axis_index(axis) % 2 == 1
        for which, low, high in ((odd, near, far), (jnp.logical_not(odd), far, near)):

            @pl.when(which)
            def _():
                lo[...] = low[...]
                hi[...] = high[...]

    copies = []
    for a in range(ca):
        own = adj[a].reshape(rows, width)
        down = adj[a - 1] if a > 0 else a_lo[0:cb]
        up = adj[a + 1] if a < ca - 1 else a_hi[0:cb]
        total = dot(own, coupling[0])
        below = pltpu.roll(dot(own, coupling[1]), 1, 0)
        above = pltpu.roll(dot(own, coupling[2]), rows - 1, 0)
        total = total + jnp.where(layer > 0, below, 0.0) + jnp.where(layer < nl - 1, above, 0.0)
        total = total + dot(down.reshape(rows, width), coupling[3])
        total = total + dot(up.reshape(rows, width), coupling[4])
        before = jnp.concatenate([b_lo[a], own[:rows - nl]], axis=0)
        behind = jnp.concatenate([own[nl:], b_hi[a]], axis=0)
        total = total + dot(before, coupling[5]) + dot(behind, coupling[6])
        held[a] = total.astype(BF16).reshape(cb, nl, width)
        copy = pltpu.make_async_copy(held.at[a], out.at[a], sems.at[a])
        copy.start()
        copies.append(copy)
    pa, pb = logf.shape[0], logf.shape[1]
    off = 8
    field[...] = jnp.zeros(field.shape, F32)
    field[2:pa + 2, off:off + pb] = logf[...]
    field[0:2, off:off + pb] = a_lo[cb:cb + 2].astype(F32)
    field[pa + 2:pa + 4, off:off + pb] = a_hi[cb:cb + 2].astype(F32)
    side_lo, side_hi = b_lo[ca].astype(F32), b_hi[ca].astype(F32)
    for r in range(pa):
        for c in range(2):
            field[r + 2, off - 2 + c:off - 1 + c] = side_lo[c * pa + r:c * pa + r + 1]
            field[r + 2, off + pb + c:off + pb + c + 1] = side_hi[c * pa + r:c * pa + r + 1]

    def stencil(ref, a, b, na, nb):
        beside = ref[a + 1:a + 1 + na, b:b + nb] + ref[a - 1:a - 1 + na, b:b + nb]
        beside = beside + ref[a:a + na, b + 1:b + 1 + nb] + ref[a:a + na, b - 1:b - 1 + nb]
        return 1.3 * ref[a:a + na, b:b + nb] - 0.2 * beside

    i, j = lax.axis_index("gx"), lax.axis_index("gy")
    last_i, last_j = lax.axis_size("gx") - 1, lax.axis_size("gy") - 1
    once[...] = jnp.zeros(once.shape, F32)
    once[1:pa + 1, off:off + pb] = stencil(field, 2, off, pa, pb)
    once[0:1, off:off + pb] = jnp.where(i > 0, stencil(field, 1, off, 1, pb), 0.0)
    once[pa + 1:pa + 2, off:off + pb] = jnp.where(i < last_i, stencil(field, pa + 2, off, 1, pb), 0.0)
    once[1:pa + 1, off - 1:off] = jnp.where(j > 0, stencil(field, 2, off - 1, pa, 1), 0.0)
    once[1:pa + 1, off + pb:off + pb + 1] = jnp.where(j < last_j, stencil(field, 2, off + pb, pa, 1), 0.0)
    prior[...] = stencil(once, 1, off, pa, pb)
    scale[...] = jnp.exp(logf[...])
    for copy in copies:
        copy.wait()


def gradient_body(got, prior, scale, out):
    owners, _, width = got.shape
    pa, pb, _ = out.shape
    slots = 16
    per_row = width // slots
    tail = got[:, slots:MSG, :].astype(F32)
    listed = [jnp.sum(tail[k:k + per_row], axis=0)[0:1] for k in range(0, owners, per_row)]
    listed = jnp.concatenate(listed, axis=1)
    node = lax.broadcasted_iota(jnp.int32, (pa * pb, owners * slots), 0).astype(F32) + 1.0
    onehot = jnp.where(node == listed, 1.0, 0.0).astype(BF16)
    blocks = got[:, 0:slots, :].reshape(owners * slots, width)
    misfit = dot(onehot, blocks).reshape(pa, pb, width)
    out[...] = scale[...] * misfit + prior[...]
    j = lax.axis_index("gy")
    for side, column in ((-1, 0), (1, pb - 1)):
        inside = jnp.logical_and(j + side >= 0, j + side < owners)
        source = jnp.clip(j + side, 0, owners - 1)
        corners = jnp.where(inside, got[source, slots:MSG, :].astype(F32) * 0.08, 0.0)
        out[0, column:column + 1] += corners[1:2]
        out[pa - 1, column:column + 1] += corners[2:3]


def cost(flops, size):
    return pl.CostEstimate(flops=flops, bytes_accessed=size, transcendentals=0)


def per_device(adjoint_trace, coupling, log_friction, send_column, live_count, target_node):
    ca, cb, nl, width = adjoint_trace.shape
    pa, pb, _ = log_friction.shape
    owners = lax.axis_size("gy")
    faces = ca * cb
    shape = jax.ShapeDtypeStruct
    wire = pltpu.CompilerParams(vmem_limit_bytes=16 * 2**20)

    to_a_far, to_a_near, to_b_far, to_b_near, blocks = pl.pallas_call(
        pack_body,
        out_shape=(
            shape((cb + 2, nl, width), BF16),
            shape((cb + 2, nl, width), BF16),
            shape((ca + 1, nl, width), BF16),
            shape((ca + 1, nl, width), BF16),
            shape(coupling.shape, BF16),
        ),
        in_specs=[HBM] * 3,
        out_specs=(VMEM,) * 5,
        scratch_shapes=[pltpu.VMEM(log_friction.shape, F32), pltpu.SemaphoreType.DMA((6,))],
        compiler_params=wire,
        name="pack",
    )(*map(in_hbm, (adjoint_trace, log_friction, coupling)))
    a_far = swap(to_a_far, "gx", 1)
    a_near = swap(to_a_near, "gx", 0)
    b_far = swap(to_b_far, "gy", 1)
    b_near = swap(to_b_near, "gy", 0)

    base, pick, ids = pl.pallas_call(
        local_body,
        out_shape=(
            shape((faces, width), F32),
            shape((faces, faces), BF16),
            shape((owners, width), F32),
        ),
        in_specs=[VMEM] * 5,
        out_specs=(VMEM,) * 3,
        scratch_shapes=[pltpu.VMEM((faces * 8, width), F32)],
        compiler_params=wire,
        cost_estimate=cost(2 * 6 * faces * width * width, 2 * 2**20),
        name="local",
    )(adjoint_trace, blocks, send_column, live_count, target_node)

    message = pl.pallas_call(
        message_body,
        out_shape=shape((owners, MSG, width), BF16),
        in_specs=[VMEM] * 8,
        out_specs=VMEM,
        scratch_shapes=[
            pltpu.VMEM((faces, width), F32),
            pltpu.VMEM((2 * (ca + cb) * 8, width), F32),
        ],
        compiler_params=wire,
        cost_estimate=cost(2 * faces * faces * width, 2**20),
        name="message",
    )(base, pick, ids, blocks, a_far, a_near, b_far, b_near)

    received = lax.all_to_all(message, "gy", split_axis=0, concat_axis=0, tiled=True)

    update, prior, scale = pl.pallas_call(
        update_body,
        out_shape=(
            shape(adjoint_trace.shape, BF16),
            shape(log_friction.shape, F32),
            shape(log_friction.shape, F32),
        ),
        in_specs=[VMEM] * 7,
        out_specs=(HBM, VMEM, VMEM),
        scratch_shapes=[
            pltpu.VMEM((cb + 2, nl, width), BF16),
            pltpu.VMEM((cb + 2, nl, width), BF16),
            pltpu.VMEM((ca + 1, nl, width), BF16),
            pltpu.VMEM((ca + 1, nl, width), BF16),
            pltpu.VMEM(adjoint_trace.shape, BF16),
            pltpu.VMEM((pa + 4, pb + 16, width), F32),
            pltpu.VMEM((pa + 2, pb + 16, width), F32),
            pltpu.SemaphoreType.DMA((ca,)),
        ],
        compiler_params=wire,
        cost_estimate=cost(2 * 7 * faces * nl * width * width, 4 * 2**20),
        name="update",
    )(adjoint_trace, blocks, log_friction, a_far, a_near, b_far, b_near)

    gradient = pl.pallas_call(
        gradient_body,
        out_shape=shape(log_friction.shape, F32),
        in_specs=[VMEM] * 3,
        out_specs=VMEM,
        compiler_params=wire,
        cost_estimate=cost(2 * pa * pb * faces * width, 2**19),
        name="gradient",
    )(received, prior, scale)
    return update, gradient


def solution(mesh):
    in_specs = (
        P("gx", "gy", None, None),
        P(),
        P("gx", "gy", None),
        P("gx", "gy", None),
        P("gx", "gy", None),
        P("gx", "gy", None, None),
    )
    out_specs = (P("gx", "gy", None, None), P("gx", "gy", None))
    return jax.shard_map(
        per_device, mesh=mesh, in_specs=in_specs, out_specs=out_specs, check_vma=False
    )
```

```python
import jax
import jax.numpy as jnp
from jax import lax
from jax.experimental import pallas as pl
from jax.experimental.pallas import tpu as pltpu
from jax.sharding import PartitionSpec as P

F32 = jnp.float32
BF16 = jnp.bfloat16
VMEM = pl.BlockSpec(memory_space=pltpu.VMEM)
HBM = pl.BlockSpec(memory_space=pltpu.HBM)
MSG = 20


def dot(a, b):
    return jnp.dot(a, b, preferred_element_type=F32)


def in_hbm(array):
    return pltpu.with_memory_space_constraint(array, pltpu.HBM)


def swap(block, axis, first):
    count = lax.axis_size(axis)
    pairs = [(i, i + 1) for i in range(first, count - 1, 2)]
    return lax.ppermute(block, axis, pairs + [(j, i) for i, j in pairs])


def pack_body(adj_hbm, logf_hbm, coupling_hbm, to_a_far, to_a_near, to_b_far, to_b_near, coupling,
              logf, sems):
    ca, cb = adj_hbm.shape[0], adj_hbm.shape[1]
    pa, pb, _ = logf.shape
    odd_a, odd_b = lax.axis_index("gx") % 2, lax.axis_index("gy") % 2
    near_a, near_b = (ca - 1) * (1 - odd_a), (cb - 1) * (1 - odd_b)
    row = (pa - 2) * (1 - odd_a)
    fields = pltpu.make_async_copy(logf_hbm, logf, sems.at[0])
    copies = [
        pltpu.make_async_copy(source, target, sems.at[1 + k])
        for k, (source, target) in enumerate(
            (
                (adj_hbm.at[ca - 1 - near_a], to_a_far.at[pl.ds(0, cb)]),
                (adj_hbm.at[near_a], to_a_near.at[pl.ds(0, cb)]),
                (adj_hbm.at[:, cb - 1 - near_b], to_b_far.at[pl.ds(0, ca)]),
                (adj_hbm.at[:, near_b], to_b_near.at[pl.ds(0, ca)]),
                (coupling_hbm, coupling),
            )
        )
    ]
    fields.start()
    for copy in copies:
        copy.start()
    fields.wait()
    to_a_far[cb:cb + 2] = logf[pl.ds(pa - 2 - row, 2)].astype(BF16)
    to_a_near[cb:cb + 2] = logf[pl.ds(row, 2)].astype(BF16)
    hi = jnp.concatenate([logf[:, pb - 2, :], logf[:, pb - 1, :]], axis=0)
    lo = jnp.concatenate([logf[:, 0, :], logf[:, 1, :]], axis=0)
    to_b_far[ca] = jnp.where(odd_b == 1, hi, lo).astype(BF16)
    to_b_near[ca] = jnp.where(odd_b == 1, lo, hi).astype(BF16)
    for copy in copies:
        copy.wait()


def local_body(adj, coupling, send, live, nodes, base, pick, ids, wide):
    ca, cb, nl, width = adj.shape
    faces = ca * cb
    for a in range(ca):
        wide[a * cb * 8:(a + 1) * cb * 8] = adj[a, :, 0:8, :].astype(F32).reshape(cb * 8, width)
    low = wide[pl.ds(0, faces, stride=8), :].astype(BF16)
    above = wide[pl.ds(1, faces, stride=8), :].astype(BF16)
    total = dot(low, coupling[0]) + dot(above, coupling[2])
    zeros = jnp.zeros((cb, width), F32)
    total = total + jnp.concatenate([zeros, dot(low[:faces - cb], coupling[3])], axis=0)
    total = total + jnp.concatenate([dot(low[cb:], coupling[4]), zeros], axis=0)
    column = lax.broadcasted_iota(jnp.int32, (faces, width), 0) % cb
    before = pltpu.roll(dot(low, coupling[5]), 1, 0)
    after = pltpu.roll(dot(low, coupling[6]), faces - 1, 0)
    total = total + jnp.where(column > 0, before, 0.0) + jnp.where(column < cb - 1, after, 0.0)
    base[...] = total
    face = lax.broadcasted_iota(jnp.int32, (faces, faces), 0)
    pick[...] = jnp.where(send[0] == face, 1.0, 0.0).T.astype(BF16)
    owners, slots = nodes.shape[2], nodes.shape[3]
    sub = lax.broadcasted_iota(jnp.int32, (slots, width), 0)
    lane = lax.broadcasted_iota(jnp.int32, (slots, width), 1)
    spread = jnp.where(lane % slots == sub, 1.0, 0.0).astype(BF16)
    listed = dot(nodes[0, 0].astype(F32).astype(BF16), spread) + 1.0
    owner = lax.broadcasted_iota(jnp.int32, (owners, owners), 0)
    other = lax.broadcasted_iota(jnp.int32, (owners, owners), 1)
    counts = jnp.sum(jnp.where(owner == other, live[0].astype(F32), 0.0), axis=1, keepdims=True)
    lane = lax.broadcasted_iota(jnp.int32, (owners, width), 1)
    mine = lane // slots == lax.axis_index("gy") % (width // slots)
    alive = (lane % slots).astype(F32) < counts
    ids[...] = jnp.where(jnp.logical_and(mine, alive), listed, 0.0)


def message_body(base, pick, ids, coupling, a_far, a_near, b_far, b_near, out, total, wide):
    faces, width = base.shape
    owners, slots = out.shape[0], faces // out.shape[0]
    cb = a_far.shape[0] - 2
    ca = b_far.shape[0] - 1
    here = lax.axis_index("gy")
    odd_a, odd_b = lax.axis_index("gx") % 2 == 1, here % 2 == 1
    for k, halo in enumerate((a_far, a_near, b_far, b_near)):
        rows = cb if k < 2 else ca
        wide[k * rows * 8:(k + 1) * rows * 8] = (
            halo[0:rows, 0:8, :].astype(F32).reshape(rows * 8, width)
        )

    def row(k, rows):
        return wide[pl.ds(k * rows * 8, rows, stride=8), :]

    def edge(k, rows):
        odd = odd_a if k < 2 else odd_b
        return jnp.where(odd, row(k ^ 1, rows), row(k, rows)).astype(BF16)

    total[...] = base[...]
    total[0:cb] += dot(edge(0, cb), coupling[3])
    total[faces - cb:faces] += dot(edge(1, cb), coupling[4])
    total[pl.ds(0, ca, stride=cb), :] += dot(edge(2, ca), coupling[5])
    total[pl.ds(cb - 1, ca, stride=cb), :] += dot(edge(3, ca), coupling[6])
    picked = dot(pick[...], total[...].astype(BF16)).astype(BF16)
    pb = a_far.shape[1]
    top = jnp.where(odd_a, a_near[cb + 1].astype(F32), a_far[cb + 1].astype(F32))
    bottom = jnp.where(odd_a, a_far[cb].astype(F32), a_near[cb].astype(F32))
    sub = lax.broadcasted_iota(jnp.int32, (MSG - slots, width), 0)

    def extra(o, column):
        rows = jnp.where(sub == 0, ids[o:o + 1, :], 0.0)
        rows = jnp.where(sub == 1, top[column:column + 1, :], rows)
        return jnp.where(sub == 2, bottom[column:column + 1, :], rows)

    for o in range(owners):
        out[o, 0:slots // 2] = picked[o * slots:(o + 1) * slots].reshape(slots // 2, 2, width)
        rest = jnp.where(o > here, extra(o, pb - 1), extra(o, 0)).astype(BF16)
        out[o, slots // 2:MSG // 2] = rest.reshape((MSG - slots) // 2, 2, width)


def update_body(adj, coupling, logf, a_far, a_near, b_far, b_near, out, prior, scale,
                a_lo, a_hi, b_lo, b_hi, held, field, once, sems):
    ca, cb, nl, width = adj.shape
    rows = cb * nl
    layer = lax.broadcasted_iota(jnp.int32, (rows, width), 0) % nl
    for axis, far, near, lo, hi in (
        ("gx", a_far, a_near, a_lo, a_hi), ("gy", b_far, b_near, b_lo, b_hi)
    ):
        odd = lax.axis_index(axis) % 2 == 1
        for which, low, high in ((odd, near, far), (jnp.logical_not(odd), far, near)):

            @pl.when(which)
            def _():
                lo[...] = low[...]
                hi[...] = high[...]

    copies = []
    for a in range(ca):
        own = adj[a].reshape(rows, width)
        down = adj[a - 1] if a > 0 else a_lo[0:cb]
        up = adj[a + 1] if a < ca - 1 else a_hi[0:cb]
        total = dot(own, coupling[0])
        below = pltpu.roll(dot(own, coupling[1]), 1, 0)
        above = pltpu.roll(dot(own, coupling[2]), rows - 1, 0)
        total = total + jnp.where(layer > 0, below, 0.0) + jnp.where(layer < nl - 1, above, 0.0)
        total = total + dot(down.reshape(rows, width), coupling[3])
        total = total + dot(up.reshape(rows, width), coupling[4])
        before = jnp.concatenate([b_lo[a], own[:rows - nl]], axis=0)
        behind = jnp.concatenate([own[nl:], b_hi[a]], axis=0)
        total = total + dot(before, coupling[5]) + dot(behind, coupling[6])
        held[a] = total.astype(BF16).reshape(cb, nl, width)
        copy = pltpu.make_async_copy(held.at[a], out.at[a], sems.at[a])
        copy.start()
        copies.append(copy)
    pa, pb = logf.shape[0], logf.shape[1]
    off = 8
    field[...] = jnp.zeros(field.shape, F32)
    field[2:pa + 2, off:off + pb] = logf[...]
    field[0:2, off:off + pb] = a_lo[cb:cb + 2].astype(F32)
    field[pa + 2:pa + 4, off:off + pb] = a_hi[cb:cb + 2].astype(F32)
    side_lo, side_hi = b_lo[ca].astype(F32), b_hi[ca].astype(F32)
    for r in range(pa):
        for c in range(2):
            field[r + 2, off - 2 + c:off - 1 + c] = side_lo[c * pa + r:c * pa + r + 1]
            field[r + 2, off + pb + c:off + pb + c + 1] = side_hi[c * pa + r:c * pa + r + 1]

    def stencil(ref, a, b, na, nb):
        beside = ref[a + 1:a + 1 + na, b:b + nb] + ref[a - 1:a - 1 + na, b:b + nb]
        beside = beside + ref[a:a + na, b + 1:b + 1 + nb] + ref[a:a + na, b - 1:b - 1 + nb]
        return 1.3 * ref[a:a + na, b:b + nb] - 0.2 * beside

    i, j = lax.axis_index("gx"), lax.axis_index("gy")
    last_i, last_j = lax.axis_size("gx") - 1, lax.axis_size("gy") - 1
    once[...] = jnp.zeros(once.shape, F32)
    once[1:pa + 1, off:off + pb] = stencil(field, 2, off, pa, pb)
    once[0:1, off:off + pb] = jnp.where(i > 0, stencil(field, 1, off, 1, pb), 0.0)
    once[pa + 1:pa + 2, off:off + pb] = jnp.where(i < last_i, stencil(field, pa + 2, off, 1, pb), 0.0)
    once[1:pa + 1, off - 1:off] = jnp.where(j > 0, stencil(field, 2, off - 1, pa, 1), 0.0)
    once[1:pa + 1, off + pb:off + pb + 1] = jnp.where(j < last_j, stencil(field, 2, off + pb, pa, 1), 0.0)
    prior[...] = stencil(once, 1, off, pa, pb)
    scale[...] = jnp.exp(logf[...])
    for copy in copies:
        copy.wait()


def gradient_body(got, prior, scale, out):
    owners, _, _, width = got.shape
    pa, pb, _ = out.shape
    slots = 16
    per_row = width // slots
    tail = got[:, slots // 2:MSG // 2].reshape(owners, MSG - slots, width).astype(F32)
    listed = [jnp.sum(tail[k:k + per_row], axis=0)[0:1] for k in range(0, owners, per_row)]
    listed = jnp.concatenate(listed, axis=1)
    node = lax.broadcasted_iota(jnp.int32, (pa * pb, owners * slots), 0).astype(F32) + 1.0
    onehot = jnp.where(node == listed, 1.0, 0.0).astype(BF16)
    blocks = got[:, 0:slots // 2].reshape(owners * slots, width)
    misfit = dot(onehot, blocks).reshape(pa, pb, width)
    out[...] = scale[...] * misfit + prior[...]
    j = lax.axis_index("gy")
    for side, column in ((-1, 0), (1, pb - 1)):
        inside = jnp.logical_and(j + side >= 0, j + side < owners)
        source = jnp.clip(j + side, 0, owners - 1)
        corners = jnp.where(inside, got[source, slots // 2:MSG // 2].reshape(MSG - slots, width).astype(F32) * 0.08, 0.0)
        out[0, column:column + 1] += corners[1:2]
        out[pa - 1, column:column + 1] += corners[2:3]


def cost(flops, size):
    return pl.CostEstimate(flops=flops, bytes_accessed=size, transcendentals=0)


def per_device(adjoint_trace, coupling, log_friction, send_column, live_count, target_node):
    ca, cb, nl, width = adjoint_trace.shape
    pa, pb, _ = log_friction.shape
    owners = lax.axis_size("gy")
    faces = ca * cb
    shape = jax.ShapeDtypeStruct
    wire = pltpu.CompilerParams(vmem_limit_bytes=16 * 2**20)

    to_a_far, to_a_near, to_b_far, to_b_near, blocks = pl.pallas_call(
        pack_body,
        out_shape=(
            shape((cb + 2, nl, width), BF16),
            shape((cb + 2, nl, width), BF16),
            shape((ca + 1, nl, width), BF16),
            shape((ca + 1, nl, width), BF16),
            shape(coupling.shape, BF16),
        ),
        in_specs=[HBM] * 3,
        out_specs=(VMEM,) * 5,
        scratch_shapes=[pltpu.VMEM(log_friction.shape, F32), pltpu.SemaphoreType.DMA((6,))],
        compiler_params=wire,
        name="pack",
    )(*map(in_hbm, (adjoint_trace, log_friction, coupling)))
    a_near = swap(to_a_near, "gx", 0)
    a_far = swap(to_a_far, "gx", 1)
    b_far = swap(to_b_far, "gy", 1)
    b_near = swap(to_b_near, "gy", 0)

    base, pick, ids = pl.pallas_call(
        local_body,
        out_shape=(
            shape((faces, width), F32),
            shape((faces, faces), BF16),
            shape((owners, width), F32),
        ),
        in_specs=[VMEM] * 5,
        out_specs=(VMEM,) * 3,
        scratch_shapes=[pltpu.VMEM((faces * 8, width), F32)],
        compiler_params=wire,
        cost_estimate=cost(2 * 6 * faces * width * width, 2 * 2**20),
        name="local",
    )(adjoint_trace, blocks, send_column, live_count, target_node)

    message = pl.pallas_call(
        message_body,
        out_shape=shape((owners, MSG // 2, 2, width), BF16),
        in_specs=[VMEM] * 8,
        out_specs=VMEM,
        scratch_shapes=[
            pltpu.VMEM((faces, width), F32),
            pltpu.VMEM((2 * (ca + cb) * 8, width), F32),
        ],
        compiler_params=wire,
        cost_estimate=cost(2 * faces * faces * width, 2**20),
        name="message",
    )(base, pick, ids, blocks, a_far, a_near, b_far, b_near)

    received = lax.all_to_all(message, "gy", split_axis=0, concat_axis=0, tiled=True)

    update, prior, scale = pl.pallas_call(
        update_body,
        out_shape=(
            shape(adjoint_trace.shape, BF16),
            shape(log_friction.shape, F32),
            shape(log_friction.shape, F32),
        ),
        in_specs=[VMEM] * 7,
        out_specs=(HBM, VMEM, VMEM),
        scratch_shapes=[
            pltpu.VMEM((cb + 2, nl, width), BF16),
            pltpu.VMEM((cb + 2, nl, width), BF16),
            pltpu.VMEM((ca + 1, nl, width), BF16),
            pltpu.VMEM((ca + 1, nl, width), BF16),
            pltpu.VMEM(adjoint_trace.shape, BF16),
            pltpu.VMEM((pa + 4, pb + 16, width), F32),
            pltpu.VMEM((pa + 2, pb + 16, width), F32),
            pltpu.SemaphoreType.DMA((ca,)),
        ],
        compiler_params=wire,
        cost_estimate=cost(2 * 7 * faces * nl * width * width, 4 * 2**20),
        name="update",
    )(adjoint_trace, blocks, log_friction, a_far, a_near, b_far, b_near)

    gradient = pl.pallas_call(
        gradient_body,
        out_shape=shape(log_friction.shape, F32),
        in_specs=[VMEM] * 3,
        out_specs=VMEM,
        compiler_params=wire,
        cost_estimate=cost(2 * pa * pb * faces * width, 2**19),
        name="gradient",
    )(received, prior, scale)
    return update, gradient


def solution(mesh):
    in_specs = (
        P("gx", "gy", None, None),
        P(),
        P("gx", "gy", None),
        P("gx", "gy", None),
        P("gx", "gy", None),
        P("gx", "gy", None, None),
    )
    out_specs = (P("gx", "gy", None, None), P("gx", "gy", None))
    return jax.shard_map(
        per_device, mesh=mesh, in_specs=in_specs, out_specs=out_specs, check_vma=False
    )
```

```python
import jax
import jax.numpy as jnp
from jax import lax
from jax.experimental import pallas as pl
from jax.experimental.pallas import tpu as pltpu
from jax.sharding import PartitionSpec as P

F32 = jnp.float32
BF16 = jnp.bfloat16
VMEM = pl.BlockSpec(memory_space=pltpu.VMEM)
HBM = pl.BlockSpec(memory_space=pltpu.HBM)
MSG = 20


def dot(a, b):
    return jnp.dot(a, b, preferred_element_type=F32)


def in_hbm(array):
    return pltpu.with_memory_space_constraint(array, pltpu.HBM)


def swap(block, axis, first):
    count = lax.axis_size(axis)
    pairs = [(i, i + 1) for i in range(first, count - 1, 2)]
    return lax.ppermute(block, axis, pairs + [(j, i) for i, j in pairs])


def pack_body(adj_hbm, logf_hbm, coupling_hbm, to_a_near, to_a_far, to_b_far, to_b_near, coupling,
              logf, sems):
    ca, cb = adj_hbm.shape[0], adj_hbm.shape[1]
    pa, pb, _ = logf.shape
    odd_a, odd_b = lax.axis_index("gx") % 2, lax.axis_index("gy") % 2
    near_a, near_b = (ca - 1) * (1 - odd_a), (cb - 1) * (1 - odd_b)
    row = (pa - 2) * (1 - odd_a)
    fields = pltpu.make_async_copy(logf_hbm, logf, sems.at[0])
    copies = [
        pltpu.make_async_copy(source, target, sems.at[1 + k])
        for k, (source, target) in enumerate(
            (
                (adj_hbm.at[ca - 1 - near_a], to_a_far.at[pl.ds(0, cb)]),
                (adj_hbm.at[near_a], to_a_near.at[pl.ds(0, cb)]),
                (adj_hbm.at[:, cb - 1 - near_b], to_b_far.at[pl.ds(0, ca)]),
                (adj_hbm.at[:, near_b], to_b_near.at[pl.ds(0, ca)]),
                (coupling_hbm, coupling),
            )
        )
    ]
    fields.start()
    for copy in copies:
        copy.start()
    fields.wait()
    to_a_far[cb:cb + 2] = logf[pl.ds(pa - 2 - row, 2)].astype(BF16)
    to_a_near[cb:cb + 2] = logf[pl.ds(row, 2)].astype(BF16)
    hi = jnp.concatenate([logf[:, pb - 2, :], logf[:, pb - 1, :]], axis=0)
    lo = jnp.concatenate([logf[:, 0, :], logf[:, 1, :]], axis=0)
    to_b_far[ca] = jnp.where(odd_b == 1, hi, lo).astype(BF16)
    to_b_near[ca] = jnp.where(odd_b == 1, lo, hi).astype(BF16)
    for copy in copies:
        copy.wait()


def local_body(adj, coupling, send, live, nodes, base, pick, ids, wide):
    ca, cb, nl, width = adj.shape
    faces = ca * cb
    for a in range(ca):
        wide[a * cb * 8:(a + 1) * cb * 8] = adj[a, :, 0:8, :].astype(F32).reshape(cb * 8, width)
    low = wide[pl.ds(0, faces, stride=8), :].astype(BF16)
    above = wide[pl.ds(1, faces, stride=8), :].astype(BF16)
    total = dot(low, coupling[0]) + dot(above, coupling[2])
    zeros = jnp.zeros((cb, width), F32)
    total = total + jnp.concatenate([zeros, dot(low[:faces - cb], coupling[3])], axis=0)
    total = total + jnp.concatenate([dot(low[cb:], coupling[4]), zeros], axis=0)
    column = lax.broadcasted_iota(jnp.int32, (faces, width), 0) % cb
    before = pltpu.roll(dot(low, coupling[5]), 1, 0)
    after = pltpu.roll(dot(low, coupling[6]), faces - 1, 0)
    total = total + jnp.where(column > 0, before, 0.0) + jnp.where(column < cb - 1, after, 0.0)
    base[...] = total
    face = lax.broadcasted_iota(jnp.int32, (faces, faces), 0)
    pick[...] = jnp.where(send[0] == face, 1.0, 0.0).T.astype(BF16)
    owners, slots = nodes.shape[2], nodes.shape[3]
    sub = lax.broadcasted_iota(jnp.int32, (slots, width), 0)
    lane = lax.broadcasted_iota(jnp.int32, (slots, width), 1)
    spread = jnp.where(lane % slots == sub, 1.0, 0.0).astype(BF16)
    listed = dot(nodes[0, 0].astype(F32).astype(BF16), spread) + 1.0
    owner = lax.broadcasted_iota(jnp.int32, (owners, owners), 0)
    other = lax.broadcasted_iota(jnp.int32, (owners, owners), 1)
    counts = jnp.sum(jnp.where(owner == other, live[0].astype(F32), 0.0), axis=1, keepdims=True)
    lane = lax.broadcasted_iota(jnp.int32, (owners, width), 1)
    mine = lane // slots == lax.axis_index("gy") % (width // slots)
    alive = (lane % slots).astype(F32) < counts
    ids[...] = jnp.where(jnp.logical_and(mine, alive), listed, 0.0)


def message_body(base, pick, ids, coupling, a_near, a_far, b_far, b_near, out, total, wide):
    faces, width = base.shape
    owners, slots = out.shape[0], faces // out.shape[0]
    cb = a_far.shape[0] - 2
    ca = b_far.shape[0] - 1
    here = lax.axis_index("gy")
    odd_a, odd_b = lax.axis_index("gx") % 2 == 1, here % 2 == 1
    for k, halo in enumerate((a_far, a_near, b_far, b_near)):
        rows = cb if k < 2 else ca
        wide[k * rows * 8:(k + 1) * rows * 8] = (
            halo[0:rows, 0:8, :].astype(F32).reshape(rows * 8, width)
        )

    def row(k, rows):
        return wide[pl.ds(k * rows * 8, rows, stride=8), :]

    def edge(k, rows):
        odd = odd_a if k < 2 else odd_b
        return jnp.where(odd, row(k ^ 1, rows), row(k, rows)).astype(BF16)

    total[...] = base[...]
    total[0:cb] += dot(edge(0, cb), coupling[3])
    total[faces - cb:faces] += dot(edge(1, cb), coupling[4])
    total[pl.ds(0, ca, stride=cb), :] += dot(edge(2, ca), coupling[5])
    total[pl.ds(cb - 1, ca, stride=cb), :] += dot(edge(3, ca), coupling[6])
    picked = dot(pick[...], total[...].astype(BF16)).astype(BF16)
    pb = a_far.shape[1]
    top = jnp.where(odd_a, a_near[cb + 1].astype(F32), a_far[cb + 1].astype(F32))
    bottom = jnp.where(odd_a, a_far[cb].astype(F32), a_near[cb].astype(F32))
    sub = lax.broadcasted_iota(jnp.int32, (MSG - slots, width), 0)

    def extra(o, column):
        rows = jnp.where(sub == 0, ids[o:o + 1, :], 0.0)
        rows = jnp.where(sub == 1, top[column:column + 1, :], rows)
        return jnp.where(sub == 2, bottom[column:column + 1, :], rows)

    for o in range(owners):
        out[o, 0:slots // 2] = picked[o * slots:(o + 1) * slots].reshape(slots // 2, 2, width)
        rest = jnp.where(o > here, extra(o, pb - 1), extra(o, 0)).astype(BF16)
        out[o, slots // 2:MSG // 2] = rest.reshape((MSG - slots) // 2, 2, width)


def update_body(adj, coupling, logf, a_near, a_far, b_far, b_near, out, prior, scale,
                a_lo, a_hi, b_lo, b_hi, held, field, once, sems):
    ca, cb, nl, width = adj.shape
    rows = cb * nl
    layer = lax.broadcasted_iota(jnp.int32, (rows, width), 0) % nl
    for axis, far, near, lo, hi in (
        ("gx", a_far, a_near, a_lo, a_hi), ("gy", b_far, b_near, b_lo, b_hi)
    ):
        odd = lax.axis_index(axis) % 2 == 1
        for which, low, high in ((odd, near, far), (jnp.logical_not(odd), far, near)):

            @pl.when(which)
            def _():
                lo[...] = low[...]
                hi[...] = high[...]

    copies = []
    for a in range(ca):
        own = adj[a].reshape(rows, width)
        down = adj[a - 1] if a > 0 else a_lo[0:cb]
        up = adj[a + 1] if a < ca - 1 else a_hi[0:cb]
        total = dot(own, coupling[0])
        below = pltpu.roll(dot(own, coupling[1]), 1, 0)
        above = pltpu.roll(dot(own, coupling[2]), rows - 1, 0)
        total = total + jnp.where(layer > 0, below, 0.0) + jnp.where(layer < nl - 1, above, 0.0)
        total = total + dot(down.reshape(rows, width), coupling[3])
        total = total + dot(up.reshape(rows, width), coupling[4])
        before = jnp.concatenate([b_lo[a], own[:rows - nl]], axis=0)
        behind = jnp.concatenate([own[nl:], b_hi[a]], axis=0)
        total = total + dot(before, coupling[5]) + dot(behind, coupling[6])
        held[a] = total.astype(BF16).reshape(cb, nl, width)
        copy = pltpu.make_async_copy(held.at[a], out.at[a], sems.at[a])
        copy.start()
        copies.append(copy)
    pa, pb = logf.shape[0], logf.shape[1]
    off = 8
    field[...] = jnp.zeros(field.shape, F32)
    field[2:pa + 2, off:off + pb] = logf[...]
    field[0:2, off:off + pb] = a_lo[cb:cb + 2].astype(F32)
    field[pa + 2:pa + 4, off:off + pb] = a_hi[cb:cb + 2].astype(F32)
    side_lo, side_hi = b_lo[ca].astype(F32), b_hi[ca].astype(F32)
    for r in range(pa):
        for c in range(2):
            field[r + 2, off - 2 + c:off - 1 + c] = side_lo[c * pa + r:c * pa + r + 1]
            field[r + 2, off + pb + c:off + pb + c + 1] = side_hi[c * pa + r:c * pa + r + 1]

    def stencil(ref, a, b, na, nb):
        beside = ref[a + 1:a + 1 + na, b:b + nb] + ref[a - 1:a - 1 + na, b:b + nb]
        beside = beside + ref[a:a + na, b + 1:b + 1 + nb] + ref[a:a + na, b - 1:b - 1 + nb]
        return 1.3 * ref[a:a + na, b:b + nb] - 0.2 * beside

    i, j = lax.axis_index("gx"), lax.axis_index("gy")
    last_i, last_j = lax.axis_size("gx") - 1, lax.axis_size("gy") - 1
    once[...] = jnp.zeros(once.shape, F32)
    once[1:pa + 1, off:off + pb] = stencil(field, 2, off, pa, pb)
    once[0:1, off:off + pb] = jnp.where(i > 0, stencil(field, 1, off, 1, pb), 0.0)
    once[pa + 1:pa + 2, off:off + pb] = jnp.where(i < last_i, stencil(field, pa + 2, off, 1, pb), 0.0)
    once[1:pa + 1, off - 1:off] = jnp.where(j > 0, stencil(field, 2, off - 1, pa, 1), 0.0)
    once[1:pa + 1, off + pb:off + pb + 1] = jnp.where(j < last_j, stencil(field, 2, off + pb, pa, 1), 0.0)
    prior[...] = stencil(once, 1, off, pa, pb)
    scale[...] = jnp.exp(logf[...])
    for copy in copies:
        copy.wait()


def gradient_body(got, prior, scale, out):
    owners, _, _, width = got.shape
    pa, pb, _ = out.shape
    slots = 16
    per_row = width // slots
    tail = got[:, slots // 2:MSG // 2].reshape(owners, MSG - slots, width).astype(F32)
    listed = [jnp.sum(tail[k:k + per_row], axis=0)[0:1] for k in range(0, owners, per_row)]
    listed = jnp.concatenate(listed, axis=1)
    node = lax.broadcasted_iota(jnp.int32, (pa * pb, owners * slots), 0).astype(F32) + 1.0
    onehot = jnp.where(node == listed, 1.0, 0.0).astype(BF16)
    blocks = got[:, 0:slots // 2].reshape(owners * slots, width)
    misfit = dot(onehot, blocks).reshape(pa, pb, width)
    out[...] = scale[...] * misfit + prior[...]
    j = lax.axis_index("gy")
    for side, column in ((-1, 0), (1, pb - 1)):
        inside = jnp.logical_and(j + side >= 0, j + side < owners)
        source = jnp.clip(j + side, 0, owners - 1)
        corners = jnp.where(inside, got[source, slots // 2:MSG // 2].reshape(MSG - slots, width).astype(F32) * 0.08, 0.0)
        out[0, column:column + 1] += corners[1:2]
        out[pa - 1, column:column + 1] += corners[2:3]


def cost(flops, size):
    return pl.CostEstimate(flops=flops, bytes_accessed=size, transcendentals=0)


def per_device(adjoint_trace, coupling, log_friction, send_column, live_count, target_node):
    ca, cb, nl, width = adjoint_trace.shape
    pa, pb, _ = log_friction.shape
    owners = lax.axis_size("gy")
    faces = ca * cb
    shape = jax.ShapeDtypeStruct
    wire = pltpu.CompilerParams(vmem_limit_bytes=16 * 2**20)

    to_a_near, to_a_far, to_b_far, to_b_near, blocks = pl.pallas_call(
        pack_body,
        out_shape=(
            shape((cb + 2, nl, width), BF16),
            shape((cb + 2, nl, width), BF16),
            shape((ca + 1, nl, width), BF16),
            shape((ca + 1, nl, width), BF16),
            shape(coupling.shape, BF16),
        ),
        in_specs=[HBM] * 3,
        out_specs=(VMEM,) * 5,
        scratch_shapes=[pltpu.VMEM(log_friction.shape, F32), pltpu.SemaphoreType.DMA((6,))],
        compiler_params=wire,
        name="pack",
    )(*map(in_hbm, (adjoint_trace, log_friction, coupling)))
    a_near = swap(to_a_near, "gx", 0)
    a_far = swap(to_a_far, "gx", 1)
    b_far = swap(to_b_far, "gy", 1)
    b_near = swap(to_b_near, "gy", 0)

    base, pick, ids = pl.pallas_call(
        local_body,
        out_shape=(
            shape((faces, width), F32),
            shape((faces, faces), BF16),
            shape((owners, width), F32),
        ),
        in_specs=[VMEM] * 5,
        out_specs=(VMEM,) * 3,
        scratch_shapes=[pltpu.VMEM((faces * 8, width), F32)],
        compiler_params=wire,
        cost_estimate=cost(2 * 6 * faces * width * width, 2 * 2**20),
        name="local",
    )(adjoint_trace, blocks, send_column, live_count, target_node)

    message = pl.pallas_call(
        message_body,
        out_shape=shape((owners, MSG // 2, 2, width), BF16),
        in_specs=[VMEM] * 8,
        out_specs=VMEM,
        scratch_shapes=[
            pltpu.VMEM((faces, width), F32),
            pltpu.VMEM((2 * (ca + cb) * 8, width), F32),
        ],
        compiler_params=wire,
        cost_estimate=cost(2 * faces * faces * width, 2**20),
        name="message",
    )(base, pick, ids, blocks, a_near, a_far, b_far, b_near)

    received = lax.all_to_all(message, "gy", split_axis=0, concat_axis=0, tiled=True)

    update, prior, scale = pl.pallas_call(
        update_body,
        out_shape=(
            shape(adjoint_trace.shape, BF16),
            shape(log_friction.shape, F32),
            shape(log_friction.shape, F32),
        ),
        in_specs=[VMEM] * 7,
        out_specs=(HBM, VMEM, VMEM),
        scratch_shapes=[
            pltpu.VMEM((cb + 2, nl, width), BF16),
            pltpu.VMEM((cb + 2, nl, width), BF16),
            pltpu.VMEM((ca + 1, nl, width), BF16),
            pltpu.VMEM((ca + 1, nl, width), BF16),
            pltpu.VMEM(adjoint_trace.shape, BF16),
            pltpu.VMEM((pa + 4, pb + 16, width), F32),
            pltpu.VMEM((pa + 2, pb + 16, width), F32),
            pltpu.SemaphoreType.DMA((ca,)),
        ],
        compiler_params=wire,
        cost_estimate=cost(2 * 7 * faces * nl * width * width, 4 * 2**20),
        name="update",
    )(adjoint_trace, blocks, log_friction, a_near, a_far, b_far, b_near)

    gradient = pl.pallas_call(
        gradient_body,
        out_shape=shape(log_friction.shape, F32),
        in_specs=[VMEM] * 3,
        out_specs=VMEM,
        compiler_params=wire,
        cost_estimate=cost(2 * pa * pb * faces * width, 2**19),
        name="gradient",
    )(received, prior, scale)
    return update, gradient


def solution(mesh):
    in_specs = (
        P("gx", "gy", None, None),
        P(),
        P("gx", "gy", None),
        P("gx", "gy", None),
        P("gx", "gy", None),
        P("gx", "gy", None, None),
    )
    out_specs = (P("gx", "gy", None, None), P("gx", "gy", None))
    return jax.shard_map(
        per_device, mesh=mesh, in_specs=in_specs, out_specs=out_specs, check_vma=False
    )
```

```python
import jax
import jax.numpy as jnp
from jax import lax
from jax.experimental import pallas as pl
from jax.experimental.pallas import tpu as pltpu
from jax.sharding import PartitionSpec as P

F32 = jnp.float32
BF16 = jnp.bfloat16
VMEM = pl.BlockSpec(memory_space=pltpu.VMEM)
HBM = pl.BlockSpec(memory_space=pltpu.HBM)
MSG = 20


def dot(a, b):
    return jnp.dot(a, b, preferred_element_type=F32)


def in_hbm(array):
    return pltpu.with_memory_space_constraint(array, pltpu.HBM)


def swap(block, axis, first):
    count = lax.axis_size(axis)
    pairs = [(i, i + 1) for i in range(first, count - 1, 2)]
    return lax.ppermute(block, axis, pairs + [(j, i) for i, j in pairs])


def pack_body(adj_hbm, logf_hbm, to_a_far, to_a_near, to_b_far, to_b_near, logf, sems):
    ca, cb = adj_hbm.shape[0], adj_hbm.shape[1]
    pa, pb, _ = logf.shape
    odd_a, odd_b = lax.axis_index("gx") % 2, lax.axis_index("gy") % 2
    near_a, near_b = (ca - 1) * (1 - odd_a), (cb - 1) * (1 - odd_b)
    row = (pa - 2) * (1 - odd_a)
    fields = pltpu.make_async_copy(logf_hbm, logf, sems.at[0])
    copies = [
        pltpu.make_async_copy(source, target, sems.at[1 + k])
        for k, (source, target) in enumerate(
            (
                (adj_hbm.at[ca - 1 - near_a], to_a_far.at[pl.ds(0, cb)]),
                (adj_hbm.at[near_a], to_a_near.at[pl.ds(0, cb)]),
                (adj_hbm.at[:, cb - 1 - near_b], to_b_far.at[pl.ds(0, ca)]),
                (adj_hbm.at[:, near_b], to_b_near.at[pl.ds(0, ca)]),
            )
        )
    ]
    fields.start()
    for copy in copies:
        copy.start()
    fields.wait()
    to_a_far[cb:cb + 2] = logf[pl.ds(pa - 2 - row, 2)].astype(BF16)
    to_a_near[cb:cb + 2] = logf[pl.ds(row, 2)].astype(BF16)
    hi = jnp.concatenate([logf[:, pb - 2, :], logf[:, pb - 1, :]], axis=0)
    lo = jnp.concatenate([logf[:, 0, :], logf[:, 1, :]], axis=0)
    to_b_far[ca] = jnp.where(odd_b == 1, hi, lo).astype(BF16)
    to_b_near[ca] = jnp.where(odd_b == 1, lo, hi).astype(BF16)
    for copy in copies:
        copy.wait()


def local_body(adj, coupling_hbm, send, live, nodes, base, pick, ids, coupling, wide, sem):
    fetch = pltpu.make_async_copy(coupling_hbm, coupling, sem)
    fetch.start()
    ca, cb, nl, width = adj.shape
    faces = ca * cb
    for a in range(ca):
        wide[a * cb * 8:(a + 1) * cb * 8] = adj[a, :, 0:8, :].astype(F32).reshape(cb * 8, width)
    face = lax.broadcasted_iota(jnp.int32, (faces, faces), 0)
    pick[...] = jnp.where(send[0] == face, 1.0, 0.0).T.astype(BF16)
    owners, slots = nodes.shape[2], nodes.shape[3]
    sub = lax.broadcasted_iota(jnp.int32, (slots, width), 0)
    lane = lax.broadcasted_iota(jnp.int32, (slots, width), 1)
    spread = jnp.where(lane % slots == sub, 1.0, 0.0).astype(BF16)
    listed = dot(nodes[0, 0].astype(F32).astype(BF16), spread) + 1.0
    owner = lax.broadcasted_iota(jnp.int32, (owners, owners), 0)
    other = lax.broadcasted_iota(jnp.int32, (owners, owners), 1)
    counts = jnp.sum(jnp.where(owner == other, live[0].astype(F32), 0.0), axis=1, keepdims=True)
    lane = lax.broadcasted_iota(jnp.int32, (owners, width), 1)
    mine = lane // slots == lax.axis_index("gy") % (width // slots)
    alive = (lane % slots).astype(F32) < counts
    ids[...] = jnp.where(jnp.logical_and(mine, alive), listed, 0.0)
    fetch.wait()
    low = wide[pl.ds(0, faces, stride=8), :].astype(BF16)
    above = wide[pl.ds(1, faces, stride=8), :].astype(BF16)
    total = dot(low, coupling[0]) + dot(above, coupling[2])
    zeros = jnp.zeros((cb, width), F32)
    total = total + jnp.concatenate([zeros, dot(low[:faces - cb], coupling[3])], axis=0)
    total = total + jnp.concatenate([dot(low[cb:], coupling[4]), zeros], axis=0)
    column = lax.broadcasted_iota(jnp.int32, (faces, width), 0) % cb
    before = pltpu.roll(dot(low, coupling[5]), 1, 0)
    after = pltpu.roll(dot(low, coupling[6]), faces - 1, 0)
    total = total + jnp.where(column > 0, before, 0.0) + jnp.where(column < cb - 1, after, 0.0)
    base[...] = total


def message_body(base, pick, ids, coupling, a_far, a_near, b_far, b_near, out, total, wide):
    faces, width = base.shape
    owners, slots = out.shape[0], faces // out.shape[0]
    cb = a_far.shape[0] - 2
    ca = b_far.shape[0] - 1
    here = lax.axis_index("gy")
    odd_a, odd_b = lax.axis_index("gx") % 2 == 1, here % 2 == 1
    for k, halo in enumerate((a_far, a_near, b_far, b_near)):
        rows = cb if k < 2 else ca
        wide[k * rows * 8:(k + 1) * rows * 8] = (
            halo[0:rows, 0:8, :].astype(F32).reshape(rows * 8, width)
        )

    def row(k, rows):
        return wide[pl.ds(k * rows * 8, rows, stride=8), :]

    def edge(k, rows):
        odd = odd_a if k < 2 else odd_b
        return jnp.where(odd, row(k ^ 1, rows), row(k, rows)).astype(BF16)

    total[...] = base[...]
    total[0:cb] += dot(edge(0, cb), coupling[3])
    total[faces - cb:faces] += dot(edge(1, cb), coupling[4])
    total[pl.ds(0, ca, stride=cb), :] += dot(edge(2, ca), coupling[5])
    total[pl.ds(cb - 1, ca, stride=cb), :] += dot(edge(3, ca), coupling[6])
    picked = dot(pick[...], total[...].astype(BF16)).astype(BF16)
    pb = a_far.shape[1]
    top = jnp.where(odd_a, a_near[cb + 1].astype(F32), a_far[cb + 1].astype(F32))
    bottom = jnp.where(odd_a, a_far[cb].astype(F32), a_near[cb].astype(F32))
    sub = lax.broadcasted_iota(jnp.int32, (MSG - slots, width), 0)

    def extra(o, column):
        rows = jnp.where(sub == 0, ids[o:o + 1, :], 0.0)
        rows = jnp.where(sub == 1, top[column:column + 1, :], rows)
        return jnp.where(sub == 2, bottom[column:column + 1, :], rows)

    for o in range(owners):
        out[o, 0:slots // 2] = picked[o * slots:(o + 1) * slots].reshape(slots // 2, 2, width)
        rest = jnp.where(o > here, extra(o, pb - 1), extra(o, 0)).astype(BF16)
        out[o, slots // 2:MSG // 2] = rest.reshape((MSG - slots) // 2, 2, width)


def update_body(adj, coupling, logf, a_far, a_near, b_far, b_near, out, prior, scale,
                a_lo, a_hi, b_lo, b_hi, held, field, once, sems):
    ca, cb, nl, width = adj.shape
    rows = cb * nl
    layer = lax.broadcasted_iota(jnp.int32, (rows, width), 0) % nl
    for axis, far, near, lo, hi in (
        ("gx", a_far, a_near, a_lo, a_hi), ("gy", b_far, b_near, b_lo, b_hi)
    ):
        odd = lax.axis_index(axis) % 2 == 1
        for which, low, high in ((odd, near, far), (jnp.logical_not(odd), far, near)):

            @pl.when(which)
            def _():
                lo[...] = low[...]
                hi[...] = high[...]

    copies = []
    for a in range(ca):
        own = adj[a].reshape(rows, width)
        down = adj[a - 1] if a > 0 else a_lo[0:cb]
        up = adj[a + 1] if a < ca - 1 else a_hi[0:cb]
        total = dot(own, coupling[0])
        below = pltpu.roll(dot(own, coupling[1]), 1, 0)
        above = pltpu.roll(dot(own, coupling[2]), rows - 1, 0)
        total = total + jnp.where(layer > 0, below, 0.0) + jnp.where(layer < nl - 1, above, 0.0)
        total = total + dot(down.reshape(rows, width), coupling[3])
        total = total + dot(up.reshape(rows, width), coupling[4])
        before = jnp.concatenate([b_lo[a], own[:rows - nl]], axis=0)
        behind = jnp.concatenate([own[nl:], b_hi[a]], axis=0)
        total = total + dot(before, coupling[5]) + dot(behind, coupling[6])
        held[a] = total.astype(BF16).reshape(cb, nl, width)
        copy = pltpu.make_async_copy(held.at[a], out.at[a], sems.at[a])
        copy.start()
        copies.append(copy)
    pa, pb = logf.shape[0], logf.shape[1]
    off = 8
    field[...] = jnp.zeros(field.shape, F32)
    field[2:pa + 2, off:off + pb] = logf[...]
    field[0:2, off:off + pb] = a_lo[cb:cb + 2].astype(F32)
    field[pa + 2:pa + 4, off:off + pb] = a_hi[cb:cb + 2].astype(F32)
    side_lo, side_hi = b_lo[ca].astype(F32), b_hi[ca].astype(F32)
    for r in range(pa):
        for c in range(2):
            field[r + 2, off - 2 + c:off - 1 + c] = side_lo[c * pa + r:c * pa + r + 1]
            field[r + 2, off + pb + c:off + pb + c + 1] = side_hi[c * pa + r:c * pa + r + 1]

    def stencil(ref, a, b, na, nb):
        beside = ref[a + 1:a + 1 + na, b:b + nb] + ref[a - 1:a - 1 + na, b:b + nb]
        beside = beside + ref[a:a + na, b + 1:b + 1 + nb] + ref[a:a + na, b - 1:b - 1 + nb]
        return 1.3 * ref[a:a + na, b:b + nb] - 0.2 * beside

    i, j = lax.axis_index("gx"), lax.axis_index("gy")
    last_i, last_j = lax.axis_size("gx") - 1, lax.axis_size("gy") - 1
    once[...] = jnp.zeros(once.shape, F32)
    once[1:pa + 1, off:off + pb] = stencil(field, 2, off, pa, pb)
    once[0:1, off:off + pb] = jnp.where(i > 0, stencil(field, 1, off, 1, pb), 0.0)
    once[pa + 1:pa + 2, off:off + pb] = jnp.where(i < last_i, stencil(field, pa + 2, off, 1, pb), 0.0)
    once[1:pa + 1, off - 1:off] = jnp.where(j > 0, stencil(field, 2, off - 1, pa, 1), 0.0)
    once[1:pa + 1, off + pb:off + pb + 1] = jnp.where(j < last_j, stencil(field, 2, off + pb, pa, 1), 0.0)
    prior[...] = stencil(once, 1, off, pa, pb)
    scale[...] = jnp.exp(logf[...])
    for copy in copies:
        copy.wait()


def gradient_body(got, prior, scale, out):
    owners, _, _, width = got.shape
    pa, pb, _ = out.shape
    slots = 16
    per_row = width // slots
    tail = got[:, slots // 2:MSG // 2].reshape(owners, MSG - slots, width).astype(F32)
    listed = [jnp.sum(tail[k:k + per_row], axis=0)[0:1] for k in range(0, owners, per_row)]
    listed = jnp.concatenate(listed, axis=1)
    node = lax.broadcasted_iota(jnp.int32, (pa * pb, owners * slots), 0).astype(F32) + 1.0
    onehot = jnp.where(node == listed, 1.0, 0.0).astype(BF16)
    blocks = got[:, 0:slots // 2].reshape(owners * slots, width)
    misfit = dot(onehot, blocks).reshape(pa, pb, width)
    out[...] = scale[...] * misfit + prior[...]
    j = lax.axis_index("gy")
    for side, column in ((-1, 0), (1, pb - 1)):
        inside = jnp.logical_and(j + side >= 0, j + side < owners)
        source = jnp.clip(j + side, 0, owners - 1)
        corners = jnp.where(inside, got[source, slots // 2:MSG // 2].reshape(MSG - slots, width).astype(F32) * 0.08, 0.0)
        out[0, column:column + 1] += corners[1:2]
        out[pa - 1, column:column + 1] += corners[2:3]


def cost(flops, size):
    return pl.CostEstimate(flops=flops, bytes_accessed=size, transcendentals=0)


def per_device(adjoint_trace, coupling, log_friction, send_column, live_count, target_node):
    ca, cb, nl, width = adjoint_trace.shape
    pa, pb, _ = log_friction.shape
    owners = lax.axis_size("gy")
    faces = ca * cb
    shape = jax.ShapeDtypeStruct
    wire = pltpu.CompilerParams(vmem_limit_bytes=16 * 2**20)

    to_a_far, to_a_near, to_b_far, to_b_near = pl.pallas_call(
        pack_body,
        out_shape=(
            shape((cb + 2, nl, width), BF16),
            shape((cb + 2, nl, width), BF16),
            shape((ca + 1, nl, width), BF16),
            shape((ca + 1, nl, width), BF16),
        ),
        in_specs=[HBM] * 2,
        out_specs=(VMEM,) * 4,
        scratch_shapes=[pltpu.VMEM(log_friction.shape, F32), pltpu.SemaphoreType.DMA((5,))],
        compiler_params=wire,
        name="pack",
    )(in_hbm(adjoint_trace), in_hbm(log_friction))
    a_near = swap(to_a_near, "gx", 0)
    a_far = swap(to_a_far, "gx", 1)
    b_far = swap(to_b_far, "gy", 1)
    b_near = swap(to_b_near, "gy", 0)

    base, pick, ids, blocks = pl.pallas_call(
        local_body,
        out_shape=(
            shape((faces, width), F32),
            shape((faces, faces), BF16),
            shape((owners, width), F32),
            shape(coupling.shape, BF16),
        ),
        in_specs=[VMEM, HBM] + [VMEM] * 3,
        out_specs=(VMEM,) * 4,
        scratch_shapes=[pltpu.VMEM((faces * 8, width), F32), pltpu.SemaphoreType.DMA],
        compiler_params=wire,
        cost_estimate=cost(2 * 6 * faces * width * width, 2 * 2**20),
        name="local",
    )(adjoint_trace, in_hbm(coupling), send_column, live_count, target_node)

    message = pl.pallas_call(
        message_body,
        out_shape=shape((owners, MSG // 2, 2, width), BF16),
        in_specs=[VMEM] * 8,
        out_specs=VMEM,
        scratch_shapes=[
            pltpu.VMEM((faces, width), F32),
            pltpu.VMEM((2 * (ca + cb) * 8, width), F32),
        ],
        compiler_params=wire,
        cost_estimate=cost(2 * faces * faces * width, 2**20),
        name="message",
    )(base, pick, ids, blocks, a_far, a_near, b_far, b_near)

    received = lax.all_to_all(message, "gy", split_axis=0, concat_axis=0, tiled=True)

    update, prior, scale = pl.pallas_call(
        update_body,
        out_shape=(
            shape(adjoint_trace.shape, BF16),
            shape(log_friction.shape, F32),
            shape(log_friction.shape, F32),
        ),
        in_specs=[VMEM] * 7,
        out_specs=(HBM, VMEM, VMEM),
        scratch_shapes=[
            pltpu.VMEM((cb + 2, nl, width), BF16),
            pltpu.VMEM((cb + 2, nl, width), BF16),
            pltpu.VMEM((ca + 1, nl, width), BF16),
            pltpu.VMEM((ca + 1, nl, width), BF16),
            pltpu.VMEM(adjoint_trace.shape, BF16),
            pltpu.VMEM((pa + 4, pb + 16, width), F32),
            pltpu.VMEM((pa + 2, pb + 16, width), F32),
            pltpu.SemaphoreType.DMA((ca,)),
        ],
        compiler_params=wire,
        cost_estimate=cost(2 * 7 * faces * nl * width * width, 4 * 2**20),
        name="update",
    )(adjoint_trace, blocks, log_friction, a_far, a_near, b_far, b_near)

    gradient = pl.pallas_call(
        gradient_body,
        out_shape=shape(log_friction.shape, F32),
        in_specs=[VMEM] * 3,
        out_specs=VMEM,
        compiler_params=wire,
        cost_estimate=cost(2 * pa * pb * faces * width, 2**19),
        name="gradient",
    )(received, prior, scale)
    return update, gradient


def solution(mesh):
    in_specs = (
        P("gx", "gy", None, None),
        P(),
        P("gx", "gy", None),
        P("gx", "gy", None),
        P("gx", "gy", None),
        P("gx", "gy", None, None),
    )
    out_specs = (P("gx", "gy", None, None), P("gx", "gy", None))
    return jax.shard_map(
        per_device, mesh=mesh, in_specs=in_specs, out_specs=out_specs, check_vma=False
    )
```

```python
import jax
import jax.numpy as jnp
from jax import lax
from jax.experimental import pallas as pl
from jax.experimental.pallas import tpu as pltpu
from jax.sharding import PartitionSpec as P

F32 = jnp.float32
BF16 = jnp.bfloat16
VMEM = pl.BlockSpec(memory_space=pltpu.VMEM)
HBM = pl.BlockSpec(memory_space=pltpu.HBM)
MSG = 20


def dot(a, b):
    return jnp.dot(a, b, preferred_element_type=F32)


def in_hbm(array):
    return pltpu.with_memory_space_constraint(array, pltpu.HBM)


def swap(block, axis, first):
    count = lax.axis_size(axis)
    pairs = [(i, i + 1) for i in range(first, count - 1, 2)]
    return lax.ppermute(block, axis, pairs + [(j, i) for i, j in pairs])


def pack_body(adj_hbm, logf_hbm, to_a_far, to_a_near, to_b_far, to_b_near, logf, sems):
    ca, cb = adj_hbm.shape[0], adj_hbm.shape[1]
    pa, pb, _ = logf.shape
    odd_a, odd_b = lax.axis_index("gx") % 2, lax.axis_index("gy") % 2
    near_a, near_b = (ca - 1) * (1 - odd_a), (cb - 1) * (1 - odd_b)
    row = (pa - 2) * (1 - odd_a)
    fields = pltpu.make_async_copy(logf_hbm, logf, sems.at[0])
    copies = [
        pltpu.make_async_copy(source, target, sems.at[1 + k])
        for k, (source, target) in enumerate(
            (
                (adj_hbm.at[ca - 1 - near_a], to_a_far.at[pl.ds(0, cb)]),
                (adj_hbm.at[near_a], to_a_near.at[pl.ds(0, cb)]),
                (adj_hbm.at[:, cb - 1 - near_b], to_b_far.at[pl.ds(0, ca)]),
                (adj_hbm.at[:, near_b], to_b_near.at[pl.ds(0, ca)]),
            )
        )
    ]
    fields.start()
    for copy in copies:
        copy.start()
    fields.wait()
    to_a_far[cb:cb + 2] = logf[pl.ds(pa - 2 - row, 2)].astype(BF16)
    to_a_near[cb:cb + 2] = logf[pl.ds(row, 2)].astype(BF16)
    hi = jnp.concatenate([logf[:, pb - 2, :], logf[:, pb - 1, :]], axis=0)
    lo = jnp.concatenate([logf[:, 0, :], logf[:, 1, :]], axis=0)
    to_b_far[ca] = jnp.where(odd_b == 1, hi, lo).astype(BF16)
    to_b_near[ca] = jnp.where(odd_b == 1, lo, hi).astype(BF16)
    for copy in copies:
        copy.wait()


def local_body(adj, coupling, send, live, nodes, base, pick, ids, wide):
    ca, cb, nl, width = adj.shape
    faces = ca * cb
    for a in range(ca):
        wide[a * cb * 8:(a + 1) * cb * 8] = adj[a, :, 0:8, :].astype(F32).reshape(cb * 8, width)
    face = lax.broadcasted_iota(jnp.int32, (faces, faces), 0)
    pick[...] = jnp.where(send[0] == face, 1.0, 0.0).T.astype(BF16)
    owners, slots = nodes.shape[2], nodes.shape[3]
    sub = lax.broadcasted_iota(jnp.int32, (slots, width), 0)
    lane = lax.broadcasted_iota(jnp.int32, (slots, width), 1)
    spread = jnp.where(lane % slots == sub, 1.0, 0.0).astype(BF16)
    listed = dot(nodes[0, 0].astype(F32).astype(BF16), spread) + 1.0
    owner = lax.broadcasted_iota(jnp.int32, (owners, owners), 0)
    other = lax.broadcasted_iota(jnp.int32, (owners, owners), 1)
    counts = jnp.sum(jnp.where(owner == other, live[0].astype(F32), 0.0), axis=1, keepdims=True)
    lane = lax.broadcasted_iota(jnp.int32, (owners, width), 1)
    mine = lane // slots == lax.axis_index("gy") % (width // slots)
    alive = (lane % slots).astype(F32) < counts
    ids[...] = jnp.where(jnp.logical_and(mine, alive), listed, 0.0)
    low = wide[pl.ds(0, faces, stride=8), :].astype(BF16)
    above = wide[pl.ds(1, faces, stride=8), :].astype(BF16)
    total = dot(low, coupling[0]) + dot(above, coupling[2])
    zeros = jnp.zeros((cb, width), F32)
    total = total + jnp.concatenate([zeros, dot(low[:faces - cb], coupling[3])], axis=0)
    total = total + jnp.concatenate([dot(low[cb:], coupling[4]), zeros], axis=0)
    column = lax.broadcasted_iota(jnp.int32, (faces, width), 0) % cb
    before = pltpu.roll(dot(low, coupling[5]), 1, 0)
    after = pltpu.roll(dot(low, coupling[6]), faces - 1, 0)
    total = total + jnp.where(column > 0, before, 0.0) + jnp.where(column < cb - 1, after, 0.0)
    base[...] = total


def message_body(base, pick, ids, coupling, a_far, a_near, b_far, b_near, out, total, wide):
    faces, width = base.shape
    owners, slots = out.shape[0], faces // out.shape[0]
    cb = a_far.shape[0] - 2
    ca = b_far.shape[0] - 1
    here = lax.axis_index("gy")
    odd_a, odd_b = lax.axis_index("gx") % 2 == 1, here % 2 == 1
    for k, halo in enumerate((a_far, a_near, b_far, b_near)):
        rows = cb if k < 2 else ca
        wide[k * rows * 8:(k + 1) * rows * 8] = (
            halo[0:rows, 0:8, :].astype(F32).reshape(rows * 8, width)
        )

    def row(k, rows):
        return wide[pl.ds(k * rows * 8, rows, stride=8), :]

    def edge(k, rows):
        odd = odd_a if k < 2 else odd_b
        return jnp.where(odd, row(k ^ 1, rows), row(k, rows)).astype(BF16)

    total[...] = base[...]
    total[0:cb] += dot(edge(0, cb), coupling[3])
    total[faces - cb:faces] += dot(edge(1, cb), coupling[4])
    total[pl.ds(0, ca, stride=cb), :] += dot(edge(2, ca), coupling[5])
    total[pl.ds(cb - 1, ca, stride=cb), :] += dot(edge(3, ca), coupling[6])
    picked = dot(pick[...], total[...].astype(BF16)).astype(BF16)
    pb = a_far.shape[1]
    top = jnp.where(odd_a, a_near[cb + 1].astype(F32), a_far[cb + 1].astype(F32))
    bottom = jnp.where(odd_a, a_far[cb].astype(F32), a_near[cb].astype(F32))
    sub = lax.broadcasted_iota(jnp.int32, (MSG - slots, width), 0)

    def extra(o, column):
        rows = jnp.where(sub == 0, ids[o:o + 1, :], 0.0)
        rows = jnp.where(sub == 1, top[column:column + 1, :], rows)
        return jnp.where(sub == 2, bottom[column:column + 1, :], rows)

    for o in range(owners):
        out[o, 0:slots // 2] = picked[o * slots:(o + 1) * slots].reshape(slots // 2, 2, width)
        rest = jnp.where(o > here, extra(o, pb - 1), extra(o, 0)).astype(BF16)
        out[o, slots // 2:MSG // 2] = rest.reshape((MSG - slots) // 2, 2, width)


def update_body(adj, coupling, logf, a_far, a_near, b_far, b_near, out, prior, scale,
                a_lo, a_hi, b_lo, b_hi, held, field, once, sems):
    ca, cb, nl, width = adj.shape
    rows = cb * nl
    layer = lax.broadcasted_iota(jnp.int32, (rows, width), 0) % nl
    for axis, far, near, lo, hi in (
        ("gx", a_far, a_near, a_lo, a_hi), ("gy", b_far, b_near, b_lo, b_hi)
    ):
        odd = lax.axis_index(axis) % 2 == 1
        for which, low, high in ((odd, near, far), (jnp.logical_not(odd), far, near)):

            @pl.when(which)
            def _():
                lo[...] = low[...]
                hi[...] = high[...]

    copies = []
    for a in range(ca):
        own = adj[a].reshape(rows, width)
        down = adj[a - 1] if a > 0 else a_lo[0:cb]
        up = adj[a + 1] if a < ca - 1 else a_hi[0:cb]
        total = dot(own, coupling[0])
        below = pltpu.roll(dot(own, coupling[1]), 1, 0)
        above = pltpu.roll(dot(own, coupling[2]), rows - 1, 0)
        total = total + jnp.where(layer > 0, below, 0.0) + jnp.where(layer < nl - 1, above, 0.0)
        total = total + dot(down.reshape(rows, width), coupling[3])
        total = total + dot(up.reshape(rows, width), coupling[4])
        before = jnp.concatenate([b_lo[a], own[:rows - nl]], axis=0)
        behind = jnp.concatenate([own[nl:], b_hi[a]], axis=0)
        total = total + dot(before, coupling[5]) + dot(behind, coupling[6])
        held[a] = total.astype(BF16).reshape(cb, nl, width)
        copy = pltpu.make_async_copy(held.at[a], out.at[a], sems.at[a])
        copy.start()
        copies.append(copy)
    pa, pb = logf.shape[0], logf.shape[1]
    off = 8
    field[...] = jnp.zeros(field.shape, F32)
    field[2:pa + 2, off:off + pb] = logf[...]
    field[0:2, off:off + pb] = a_lo[cb:cb + 2].astype(F32)
    field[pa + 2:pa + 4, off:off + pb] = a_hi[cb:cb + 2].astype(F32)
    side_lo, side_hi = b_lo[ca].astype(F32), b_hi[ca].astype(F32)
    for r in range(pa):
        for c in range(2):
            field[r + 2, off - 2 + c:off - 1 + c] = side_lo[c * pa + r:c * pa + r + 1]
            field[r + 2, off + pb + c:off + pb + c + 1] = side_hi[c * pa + r:c * pa + r + 1]

    def stencil(ref, a, b, na, nb):
        beside = ref[a + 1:a + 1 + na, b:b + nb] + ref[a - 1:a - 1 + na, b:b + nb]
        beside = beside + ref[a:a + na, b + 1:b + 1 + nb] + ref[a:a + na, b - 1:b - 1 + nb]
        return 1.3 * ref[a:a + na, b:b + nb] - 0.2 * beside

    i, j = lax.axis_index("gx"), lax.axis_index("gy")
    last_i, last_j = lax.axis_size("gx") - 1, lax.axis_size("gy") - 1
    once[...] = jnp.zeros(once.shape, F32)
    once[1:pa + 1, off:off + pb] = stencil(field, 2, off, pa, pb)
    once[0:1, off:off + pb] = jnp.where(i > 0, stencil(field, 1, off, 1, pb), 0.0)
    once[pa + 1:pa + 2, off:off + pb] = jnp.where(i < last_i, stencil(field, pa + 2, off, 1, pb), 0.0)
    once[1:pa + 1, off - 1:off] = jnp.where(j > 0, stencil(field, 2, off - 1, pa, 1), 0.0)
    once[1:pa + 1, off + pb:off + pb + 1] = jnp.where(j < last_j, stencil(field, 2, off + pb, pa, 1), 0.0)
    prior[...] = stencil(once, 1, off, pa, pb)
    scale[...] = jnp.exp(logf[...])
    for copy in copies:
        copy.wait()


def gradient_body(got, prior, scale, out):
    owners, _, _, width = got.shape
    pa, pb, _ = out.shape
    slots = 16
    per_row = width // slots
    tail = got[:, slots // 2:MSG // 2].reshape(owners, MSG - slots, width).astype(F32)
    listed = [jnp.sum(tail[k:k + per_row], axis=0)[0:1] for k in range(0, owners, per_row)]
    listed = jnp.concatenate(listed, axis=1)
    node = lax.broadcasted_iota(jnp.int32, (pa * pb, owners * slots), 0).astype(F32) + 1.0
    onehot = jnp.where(node == listed, 1.0, 0.0).astype(BF16)
    blocks = got[:, 0:slots // 2].reshape(owners * slots, width)
    misfit = dot(onehot, blocks).reshape(pa, pb, width)
    out[...] = scale[...] * misfit + prior[...]
    j = lax.axis_index("gy")
    for side, column in ((-1, 0), (1, pb - 1)):
        inside = jnp.logical_and(j + side >= 0, j + side < owners)
        source = jnp.clip(j + side, 0, owners - 1)
        corners = jnp.where(inside, got[source, slots // 2:MSG // 2].reshape(MSG - slots, width).astype(F32) * 0.08, 0.0)
        out[0, column:column + 1] += corners[1:2]
        out[pa - 1, column:column + 1] += corners[2:3]


def cost(flops, size):
    return pl.CostEstimate(flops=flops, bytes_accessed=size, transcendentals=0)


def per_device(adjoint_trace, coupling, log_friction, send_column, live_count, target_node):
    ca, cb, nl, width = adjoint_trace.shape
    pa, pb, _ = log_friction.shape
    owners = lax.axis_size("gy")
    faces = ca * cb
    shape = jax.ShapeDtypeStruct
    wire = pltpu.CompilerParams(vmem_limit_bytes=16 * 2**20)

    to_a_far, to_a_near, to_b_far, to_b_near = pl.pallas_call(
        pack_body,
        out_shape=(
            shape((cb + 2, nl, width), BF16),
            shape((cb + 2, nl, width), BF16),
            shape((ca + 1, nl, width), BF16),
            shape((ca + 1, nl, width), BF16),
        ),
        in_specs=[HBM] * 2,
        out_specs=(VMEM,) * 4,
        scratch_shapes=[pltpu.VMEM(log_friction.shape, F32), pltpu.SemaphoreType.DMA((5,))],
        compiler_params=wire,
        cost_estimate=cost(10**9, 3 * 2**20),
        name="pack",
    )(in_hbm(adjoint_trace), in_hbm(log_friction))
    a_near = swap(to_a_near, "gx", 0)
    a_far = swap(to_a_far, "gx", 1)
    b_far = swap(to_b_far, "gy", 1)
    b_near = swap(to_b_near, "gy", 0)

    base, pick, ids = pl.pallas_call(
        local_body,
        out_shape=(
            shape((faces, width), F32),
            shape((faces, faces), BF16),
            shape((owners, width), F32),
        ),
        in_specs=[VMEM] * 5,
        out_specs=(VMEM,) * 3,
        scratch_shapes=[pltpu.VMEM((faces * 8, width), F32)],
        compiler_params=wire,
        cost_estimate=cost(2 * 6 * faces * width * width, 2 * 2**20),
        name="local",
    )(adjoint_trace, coupling, send_column, live_count, target_node)

    message = pl.pallas_call(
        message_body,
        out_shape=shape((owners, MSG // 2, 2, width), BF16),
        in_specs=[VMEM] * 8,
        out_specs=VMEM,
        scratch_shapes=[
            pltpu.VMEM((faces, width), F32),
            pltpu.VMEM((2 * (ca + cb) * 8, width), F32),
        ],
        compiler_params=wire,
        cost_estimate=cost(2 * faces * faces * width, 2**20),
        name="message",
    )(base, pick, ids, coupling, a_far, a_near, b_far, b_near)

    received = lax.all_to_all(message, "gy", split_axis=0, concat_axis=0, tiled=True)

    update, prior, scale = pl.pallas_call(
        update_body,
        out_shape=(
            shape(adjoint_trace.shape, BF16),
            shape(log_friction.shape, F32),
            shape(log_friction.shape, F32),
        ),
        in_specs=[VMEM] * 7,
        out_specs=(HBM, VMEM, VMEM),
        scratch_shapes=[
            pltpu.VMEM((cb + 2, nl, width), BF16),
            pltpu.VMEM((cb + 2, nl, width), BF16),
            pltpu.VMEM((ca + 1, nl, width), BF16),
            pltpu.VMEM((ca + 1, nl, width), BF16),
            pltpu.VMEM(adjoint_trace.shape, BF16),
            pltpu.VMEM((pa + 4, pb + 16, width), F32),
            pltpu.VMEM((pa + 2, pb + 16, width), F32),
            pltpu.SemaphoreType.DMA((ca,)),
        ],
        compiler_params=wire,
        cost_estimate=cost(2 * 7 * faces * nl * width * width, 4 * 2**20),
        name="update",
    )(adjoint_trace, coupling, log_friction, a_far, a_near, b_far, b_near)

    gradient = pl.pallas_call(
        gradient_body,
        out_shape=shape(log_friction.shape, F32),
        in_specs=[VMEM] * 3,
        out_specs=VMEM,
        compiler_params=wire,
        cost_estimate=cost(2 * pa * pb * faces * width, 2**19),
        name="gradient",
    )(received, prior, scale)
    return update, gradient


def solution(mesh):
    in_specs = (
        P("gx", "gy", None, None),
        P(),
        P("gx", "gy", None),
        P("gx", "gy", None),
        P("gx", "gy", None),
        P("gx", "gy", None, None),
    )
    out_specs = (P("gx", "gy", None, None), P("gx", "gy", None))
    return jax.shard_map(
        per_device, mesh=mesh, in_specs=in_specs, out_specs=out_specs, check_vma=False
    )
```

```python
import jax
import jax.numpy as jnp
from jax import lax
from jax.experimental import pallas as pl
from jax.experimental.pallas import tpu as pltpu
from jax.sharding import PartitionSpec as P

F32 = jnp.float32
BF16 = jnp.bfloat16
VMEM = pl.BlockSpec(memory_space=pltpu.VMEM)
HBM = pl.BlockSpec(memory_space=pltpu.HBM)
MSG = 20


def dot(a, b):
    return jnp.dot(a, b, preferred_element_type=F32)


def in_hbm(array):
    return pltpu.with_memory_space_constraint(array, pltpu.HBM)


def swap(block, axis, first):
    count = lax.axis_size(axis)
    pairs = [(i, i + 1) for i in range(first, count - 1, 2)]
    return lax.ppermute(block, axis, pairs + [(j, i) for i, j in pairs])


def pack_body(adj_hbm, logf_hbm, to_a_far, to_a_near, to_b_far, to_b_near, logf, sems):
    ca, cb = adj_hbm.shape[0], adj_hbm.shape[1]
    pa, pb, _ = logf.shape
    odd_a, odd_b = lax.axis_index("gx") % 2, lax.axis_index("gy") % 2
    near_a, near_b = (ca - 1) * (1 - odd_a), (cb - 1) * (1 - odd_b)
    row = (pa - 2) * (1 - odd_a)
    fields = pltpu.make_async_copy(logf_hbm, logf, sems.at[0])
    copies = [
        pltpu.make_async_copy(source, target, sems.at[1 + k])
        for k, (source, target) in enumerate(
            (
                (adj_hbm.at[ca - 1 - near_a], to_a_far.at[pl.ds(0, cb)]),
                (adj_hbm.at[near_a], to_a_near.at[pl.ds(0, cb)]),
                (adj_hbm.at[:, cb - 1 - near_b], to_b_far.at[pl.ds(0, ca)]),
                (adj_hbm.at[:, near_b], to_b_near.at[pl.ds(0, ca)]),
            )
        )
    ]
    fields.start()
    for copy in copies:
        copy.start()
    fields.wait()
    to_a_far[cb:cb + 2] = logf[pl.ds(pa - 2 - row, 2)].astype(BF16)
    to_a_near[cb:cb + 2] = logf[pl.ds(row, 2)].astype(BF16)
    hi = jnp.concatenate([logf[:, pb - 2, :], logf[:, pb - 1, :]], axis=0)
    lo = jnp.concatenate([logf[:, 0, :], logf[:, 1, :]], axis=0)
    to_b_far[ca] = jnp.where(odd_b == 1, hi, lo).astype(BF16)
    to_b_near[ca] = jnp.where(odd_b == 1, lo, hi).astype(BF16)
    for copy in copies:
        copy.wait()


def local_body(adj, coupling, send, live, nodes, base, pick, ids, wide):
    ca, cb, nl, width = adj.shape
    faces = ca * cb
    for a in range(ca):
        wide[a * cb * 8:(a + 1) * cb * 8] = adj[a, :, 0:8, :].astype(F32).reshape(cb * 8, width)
    face = lax.broadcasted_iota(jnp.int32, (faces, faces), 0)
    pick[...] = jnp.where(send[0] == face, 1.0, 0.0).T.astype(BF16)
    owners, slots = nodes.shape[2], nodes.shape[3]
    sub = lax.broadcasted_iota(jnp.int32, (slots, width), 0)
    lane = lax.broadcasted_iota(jnp.int32, (slots, width), 1)
    spread = jnp.where(lane % slots == sub, 1.0, 0.0).astype(BF16)
    listed = dot(nodes[0, 0].astype(F32).astype(BF16), spread) + 1.0
    owner = lax.broadcasted_iota(jnp.int32, (owners, owners), 0)
    other = lax.broadcasted_iota(jnp.int32, (owners, owners), 1)
    counts = jnp.sum(jnp.where(owner == other, live[0].astype(F32), 0.0), axis=1, keepdims=True)
    lane = lax.broadcasted_iota(jnp.int32, (owners, width), 1)
    mine = lane // slots == lax.axis_index("gy") % (width // slots)
    alive = (lane % slots).astype(F32) < counts
    ids[...] = jnp.where(jnp.logical_and(mine, alive), listed, 0.0)
    low = wide[pl.ds(0, faces, stride=8), :].astype(BF16)
    above = wide[pl.ds(1, faces, stride=8), :].astype(BF16)
    total = dot(low, coupling[0]) + dot(above, coupling[2])
    zeros = jnp.zeros((cb, width), F32)
    total = total + jnp.concatenate([zeros, dot(low[:faces - cb], coupling[3])], axis=0)
    total = total + jnp.concatenate([dot(low[cb:], coupling[4]), zeros], axis=0)
    column = lax.broadcasted_iota(jnp.int32, (faces, width), 0) % cb
    before = pltpu.roll(dot(low, coupling[5]), 1, 0)
    after = pltpu.roll(dot(low, coupling[6]), faces - 1, 0)
    total = total + jnp.where(column > 0, before, 0.0) + jnp.where(column < cb - 1, after, 0.0)
    base[...] = total


def gx_edge(total, halo, wide, coupling, high):
    faces, width = total.shape
    cb = halo.shape[0] - 2
    wide[0:cb * 8] = halo[0:cb, 0:8, :].astype(F32).reshape(cb * 8, width)
    rows = pl.ds(pl.multiple_of((faces - cb) * high, cb), cb)
    total[rows, :] += dot(wide[pl.ds(0, cb, stride=8), :].astype(BF16), coupling[3 + high])


def edges_body(base, coupling, a_far, b_far, b_near, total, wide):
    faces, width = base.shape
    ca = b_far.shape[0] - 1
    cb = faces // ca
    odd_b = lax.axis_index("gy") % 2 == 1
    total[...] = base[...]
    gx_edge(total, a_far, wide, coupling, lax.axis_index("gx") % 2)
    for k, halo in enumerate((b_far, b_near)):
        wide[k * ca * 8:(k + 1) * ca * 8] = halo[0:ca, 0:8, :].astype(F32).reshape(ca * 8, width)

    def edge(k):
        own, other = (wide[pl.ds(n * ca * 8, ca, stride=8), :] for n in (k, 1 - k))
        return jnp.where(odd_b, other, own).astype(BF16)

    total[pl.ds(0, ca, stride=cb), :] += dot(edge(0), coupling[5])
    total[pl.ds(cb - 1, ca, stride=cb), :] += dot(edge(1), coupling[6])


def message_body(partial, pick, ids, coupling, a_far, a_near, out, total, wide):
    faces, width = partial.shape
    owners, slots = out.shape[0], faces // out.shape[0]
    cb = a_far.shape[0] - 2
    here = lax.axis_index("gy")
    odd_a = lax.axis_index("gx") % 2 == 1
    total[...] = partial[...]
    gx_edge(total, a_near, wide, coupling, 1 - lax.axis_index("gx") % 2)
    picked = dot(pick[...], total[...].astype(BF16)).astype(BF16)
    pb = a_far.shape[1]
    top = jnp.where(odd_a, a_near[cb + 1].astype(F32), a_far[cb + 1].astype(F32))
    bottom = jnp.where(odd_a, a_far[cb].astype(F32), a_near[cb].astype(F32))
    sub = lax.broadcasted_iota(jnp.int32, (MSG - slots, width), 0)

    def extra(o, column):
        rows = jnp.where(sub == 0, ids[o:o + 1, :], 0.0)
        rows = jnp.where(sub == 1, top[column:column + 1, :], rows)
        return jnp.where(sub == 2, bottom[column:column + 1, :], rows)

    for o in range(owners):
        out[o, 0:slots // 2] = picked[o * slots:(o + 1) * slots].reshape(slots // 2, 2, width)
        rest = jnp.where(o > here, extra(o, pb - 1), extra(o, 0)).astype(BF16)
        out[o, slots // 2:MSG // 2] = rest.reshape((MSG - slots) // 2, 2, width)


def update_body(adj, coupling, logf, a_far, a_near, b_far, b_near, out, prior, scale,
                a_lo, a_hi, b_lo, b_hi, held, field, once, sems):
    ca, cb, nl, width = adj.shape
    rows = cb * nl
    layer = lax.broadcasted_iota(jnp.int32, (rows, width), 0) % nl
    for axis, far, near, lo, hi in (
        ("gx", a_far, a_near, a_lo, a_hi), ("gy", b_far, b_near, b_lo, b_hi)
    ):
        odd = lax.axis_index(axis) % 2 == 1
        for which, low, high in ((odd, near, far), (jnp.logical_not(odd), far, near)):

            @pl.when(which)
            def _():
                lo[...] = low[...]
                hi[...] = high[...]

    copies = []
    for a in range(ca):
        own = adj[a].reshape(rows, width)
        down = adj[a - 1] if a > 0 else a_lo[0:cb]
        up = adj[a + 1] if a < ca - 1 else a_hi[0:cb]
        total = dot(own, coupling[0])
        below = pltpu.roll(dot(own, coupling[1]), 1, 0)
        above = pltpu.roll(dot(own, coupling[2]), rows - 1, 0)
        total = total + jnp.where(layer > 0, below, 0.0) + jnp.where(layer < nl - 1, above, 0.0)
        total = total + dot(down.reshape(rows, width), coupling[3])
        total = total + dot(up.reshape(rows, width), coupling[4])
        before = jnp.concatenate([b_lo[a], own[:rows - nl]], axis=0)
        behind = jnp.concatenate([own[nl:], b_hi[a]], axis=0)
        total = total + dot(before, coupling[5]) + dot(behind, coupling[6])
        held[a] = total.astype(BF16).reshape(cb, nl, width)
        copy = pltpu.make_async_copy(held.at[a], out.at[a], sems.at[a])
        copy.start()
        copies.append(copy)
    pa, pb = logf.shape[0], logf.shape[1]
    off = 8
    field[...] = jnp.zeros(field.shape, F32)
    field[2:pa + 2, off:off + pb] = logf[...]
    field[0:2, off:off + pb] = a_lo[cb:cb + 2].astype(F32)
    field[pa + 2:pa + 4, off:off + pb] = a_hi[cb:cb + 2].astype(F32)
    side_lo, side_hi = b_lo[ca].astype(F32), b_hi[ca].astype(F32)
    for r in range(pa):
        for c in range(2):
            field[r + 2, off - 2 + c:off - 1 + c] = side_lo[c * pa + r:c * pa + r + 1]
            field[r + 2, off + pb + c:off + pb + c + 1] = side_hi[c * pa + r:c * pa + r + 1]

    def stencil(ref, a, b, na, nb):
        beside = ref[a + 1:a + 1 + na, b:b + nb] + ref[a - 1:a - 1 + na, b:b + nb]
        beside = beside + ref[a:a + na, b + 1:b + 1 + nb] + ref[a:a + na, b - 1:b - 1 + nb]
        return 1.3 * ref[a:a + na, b:b + nb] - 0.2 * beside

    i, j = lax.axis_index("gx"), lax.axis_index("gy")
    last_i, last_j = lax.axis_size("gx") - 1, lax.axis_size("gy") - 1
    once[...] = jnp.zeros(once.shape, F32)
    once[1:pa + 1, off:off + pb] = stencil(field, 2, off, pa, pb)
    once[0:1, off:off + pb] = jnp.where(i > 0, stencil(field, 1, off, 1, pb), 0.0)
    once[pa + 1:pa + 2, off:off + pb] = jnp.where(i < last_i, stencil(field, pa + 2, off, 1, pb), 0.0)
    once[1:pa + 1, off - 1:off] = jnp.where(j > 0, stencil(field, 2, off - 1, pa, 1), 0.0)
    once[1:pa + 1, off + pb:off + pb + 1] = jnp.where(j < last_j, stencil(field, 2, off + pb, pa, 1), 0.0)
    prior[...] = stencil(once, 1, off, pa, pb)
    scale[...] = jnp.exp(logf[...])
    for copy in copies:
        copy.wait()


def gradient_body(got, prior, scale, out):
    owners, _, _, width = got.shape
    pa, pb, _ = out.shape
    slots = 16
    per_row = width // slots
    tail = got[:, slots // 2:MSG // 2].reshape(owners, MSG - slots, width).astype(F32)
    listed = [jnp.sum(tail[k:k + per_row], axis=0)[0:1] for k in range(0, owners, per_row)]
    listed = jnp.concatenate(listed, axis=1)
    node = lax.broadcasted_iota(jnp.int32, (pa * pb, owners * slots), 0).astype(F32) + 1.0
    onehot = jnp.where(node == listed, 1.0, 0.0).astype(BF16)
    blocks = got[:, 0:slots // 2].reshape(owners * slots, width)
    misfit = dot(onehot, blocks).reshape(pa, pb, width)
    out[...] = scale[...] * misfit + prior[...]
    j = lax.axis_index("gy")
    for side, column in ((-1, 0), (1, pb - 1)):
        inside = jnp.logical_and(j + side >= 0, j + side < owners)
        source = jnp.clip(j + side, 0, owners - 1)
        corners = jnp.where(inside, got[source, slots // 2:MSG // 2].reshape(MSG - slots, width).astype(F32) * 0.08, 0.0)
        out[0, column:column + 1] += corners[1:2]
        out[pa - 1, column:column + 1] += corners[2:3]


def cost(flops, size):
    return pl.CostEstimate(flops=flops, bytes_accessed=size, transcendentals=0)


def per_device(adjoint_trace, coupling, log_friction, send_column, live_count, target_node):
    ca, cb, nl, width = adjoint_trace.shape
    pa, pb, _ = log_friction.shape
    owners = lax.axis_size("gy")
    faces = ca * cb
    shape = jax.ShapeDtypeStruct
    wire = pltpu.CompilerParams(vmem_limit_bytes=16 * 2**20)

    to_a_far, to_a_near, to_b_far, to_b_near = pl.pallas_call(
        pack_body,
        out_shape=(
            shape((cb + 2, nl, width), BF16),
            shape((cb + 2, nl, width), BF16),
            shape((ca + 1, nl, width), BF16),
            shape((ca + 1, nl, width), BF16),
        ),
        in_specs=[HBM] * 2,
        out_specs=(VMEM,) * 4,
        scratch_shapes=[pltpu.VMEM(log_friction.shape, F32), pltpu.SemaphoreType.DMA((5,))],
        compiler_params=wire,
        cost_estimate=cost(10**9, 3 * 2**20),
        name="pack",
    )(in_hbm(adjoint_trace), in_hbm(log_friction))
    a_near = swap(to_a_near, "gx", 0)
    a_far = swap(to_a_far, "gx", 1)
    b_far = swap(to_b_far, "gy", 1)
    b_near = swap(to_b_near, "gy", 0)

    base, pick, ids = pl.pallas_call(
        local_body,
        out_shape=(
            shape((faces, width), F32),
            shape((faces, faces), BF16),
            shape((owners, width), F32),
        ),
        in_specs=[VMEM] * 5,
        out_specs=(VMEM,) * 3,
        scratch_shapes=[pltpu.VMEM((faces * 8, width), F32)],
        compiler_params=wire,
        cost_estimate=cost(2 * 6 * faces * width * width, 2 * 2**20),
        name="local",
    )(adjoint_trace, coupling, send_column, live_count, target_node)

    partial = pl.pallas_call(
        edges_body,
        out_shape=shape((faces, width), F32),
        in_specs=[VMEM] * 5,
        out_specs=VMEM,
        scratch_shapes=[pltpu.VMEM((2 * ca * 8, width), F32)],
        compiler_params=wire,
        cost_estimate=cost(2 * 3 * ca * width * width, 2**18),
        name="edges",
    )(base, coupling, a_far, b_far, b_near)

    message = pl.pallas_call(
        message_body,
        out_shape=shape((owners, MSG // 2, 2, width), BF16),
        in_specs=[VMEM] * 6,
        out_specs=VMEM,
        scratch_shapes=[
            pltpu.VMEM((faces, width), F32),
            pltpu.VMEM((cb * 8, width), F32),
        ],
        compiler_params=wire,
        cost_estimate=cost(2 * faces * faces * width, 2**20),
        name="message",
    )(partial, pick, ids, coupling, a_far, a_near)

    received = lax.all_to_all(message, "gy", split_axis=0, concat_axis=0, tiled=True)

    update, prior, scale = pl.pallas_call(
        update_body,
        out_shape=(
            shape(adjoint_trace.shape, BF16),
            shape(log_friction.shape, F32),
            shape(log_friction.shape, F32),
        ),
        in_specs=[VMEM] * 7,
        out_specs=(HBM, VMEM, VMEM),
        scratch_shapes=[
            pltpu.VMEM((cb + 2, nl, width), BF16),
            pltpu.VMEM((cb + 2, nl, width), BF16),
            pltpu.VMEM((ca + 1, nl, width), BF16),
            pltpu.VMEM((ca + 1, nl, width), BF16),
            pltpu.VMEM(adjoint_trace.shape, BF16),
            pltpu.VMEM((pa + 4, pb + 16, width), F32),
            pltpu.VMEM((pa + 2, pb + 16, width), F32),
            pltpu.SemaphoreType.DMA((ca,)),
        ],
        compiler_params=wire,
        cost_estimate=cost(2 * 7 * faces * nl * width * width, 4 * 2**20),
        name="update",
    )(adjoint_trace, coupling, log_friction, a_far, a_near, b_far, b_near)

    gradient = pl.pallas_call(
        gradient_body,
        out_shape=shape(log_friction.shape, F32),
        in_specs=[VMEM] * 3,
        out_specs=VMEM,
        compiler_params=wire,
        cost_estimate=cost(2 * pa * pb * faces * width, 2**19),
        name="gradient",
    )(received, prior, scale)
    return update, gradient


def solution(mesh):
    in_specs = (
        P("gx", "gy", None, None),
        P(),
        P("gx", "gy", None),
        P("gx", "gy", None),
        P("gx", "gy", None),
        P("gx", "gy", None, None),
    )
    out_specs = (P("gx", "gy", None, None), P("gx", "gy", None))
    return jax.shard_map(
        per_device, mesh=mesh, in_specs=in_specs, out_specs=out_specs, check_vma=False
    )
```

```python
import jax
import jax.numpy as jnp
from jax import lax
from jax.experimental import pallas as pl
from jax.experimental.pallas import tpu as pltpu
from jax.sharding import PartitionSpec as P

F32 = jnp.float32
BF16 = jnp.bfloat16
VMEM = pl.BlockSpec(memory_space=pltpu.VMEM)
HBM = pl.BlockSpec(memory_space=pltpu.HBM)
MSG = 20


def dot(a, b):
    return jnp.dot(a, b, preferred_element_type=F32)


def in_hbm(array):
    return pltpu.with_memory_space_constraint(array, pltpu.HBM)


def swap(block, axis, first):
    count = lax.axis_size(axis)
    pairs = [(i, i + 1) for i in range(first, count - 1, 2)]
    return lax.ppermute(block, axis, pairs + [(j, i) for i, j in pairs])


def pack_body(adj_hbm, logf_hbm, to_a_far, to_a_near, to_b_far, to_b_near, logf, sems):
    ca, cb = adj_hbm.shape[0], adj_hbm.shape[1]
    pa, pb, _ = logf.shape
    odd_a, odd_b = lax.axis_index("gx") % 2, lax.axis_index("gy") % 2
    near_a, near_b = (ca - 1) * (1 - odd_a), (cb - 1) * (1 - odd_b)
    row = (pa - 2) * (1 - odd_a)
    fields = pltpu.make_async_copy(logf_hbm, logf, sems.at[0])
    copies = [
        pltpu.make_async_copy(source, target, sems.at[1 + k])
        for k, (source, target) in enumerate(
            (
                (adj_hbm.at[:, cb - 1 - near_b], to_b_far.at[pl.ds(0, ca)]),
                (adj_hbm.at[:, near_b], to_b_near.at[pl.ds(0, ca)]),
                (adj_hbm.at[ca - 1 - near_a], to_a_far.at[pl.ds(0, cb)]),
                (adj_hbm.at[near_a], to_a_near.at[pl.ds(0, cb)]),
            )
        )
    ]
    fields.start()
    for copy in copies:
        copy.start()
    fields.wait()
    to_a_far[cb:cb + 2] = logf[pl.ds(pa - 2 - row, 2)].astype(BF16)
    to_a_near[cb:cb + 2] = logf[pl.ds(row, 2)].astype(BF16)
    hi = jnp.concatenate([logf[:, pb - 2, :], logf[:, pb - 1, :]], axis=0)
    lo = jnp.concatenate([logf[:, 0, :], logf[:, 1, :]], axis=0)
    to_b_far[ca] = jnp.where(odd_b == 1, hi, lo).astype(BF16)
    to_b_near[ca] = jnp.where(odd_b == 1, lo, hi).astype(BF16)
    for copy in copies:
        copy.wait()


def local_body(adj, coupling, send, live, nodes, base, pick, ids, wide):
    ca, cb, nl, width = adj.shape
    faces = ca * cb
    for a in range(ca):
        wide[a * cb * 8:(a + 1) * cb * 8] = adj[a, :, 0:8, :].astype(F32).reshape(cb * 8, width)
    face = lax.broadcasted_iota(jnp.int32, (faces, faces), 0)
    pick[...] = jnp.where(send[0] == face, 1.0, 0.0).T.astype(BF16)
    owners, slots = nodes.shape[2], nodes.shape[3]
    sub = lax.broadcasted_iota(jnp.int32, (slots, width), 0)
    lane = lax.broadcasted_iota(jnp.int32, (slots, width), 1)
    spread = jnp.where(lane % slots == sub, 1.0, 0.0).astype(BF16)
    listed = dot(nodes[0, 0].astype(F32).astype(BF16), spread) + 1.0
    owner = lax.broadcasted_iota(jnp.int32, (owners, owners), 0)
    other = lax.broadcasted_iota(jnp.int32, (owners, owners), 1)
    counts = jnp.sum(jnp.where(owner == other, live[0].astype(F32), 0.0), axis=1, keepdims=True)
    lane = lax.broadcasted_iota(jnp.int32, (owners, width), 1)
    mine = lane // slots == lax.axis_index("gy") % (width // slots)
    alive = (lane % slots).astype(F32) < counts
    ids[...] = jnp.where(jnp.logical_and(mine, alive), listed, 0.0)
    low = wide[pl.ds(0, faces, stride=8), :].astype(BF16)
    above = wide[pl.ds(1, faces, stride=8), :].astype(BF16)
    total = dot(low, coupling[0]) + dot(above, coupling[2])
    zeros = jnp.zeros((cb, width), F32)
    total = total + jnp.concatenate([zeros, dot(low[:faces - cb], coupling[3])], axis=0)
    total = total + jnp.concatenate([dot(low[cb:], coupling[4]), zeros], axis=0)
    column = lax.broadcasted_iota(jnp.int32, (faces, width), 0) % cb
    before = pltpu.roll(dot(low, coupling[5]), 1, 0)
    after = pltpu.roll(dot(low, coupling[6]), faces - 1, 0)
    total = total + jnp.where(column > 0, before, 0.0) + jnp.where(column < cb - 1, after, 0.0)
    base[...] = total


def gx_edge(total, halo, wide, coupling, high):
    faces, width = total.shape
    cb = halo.shape[0] - 2
    wide[0:cb * 8] = halo[0:cb, 0:8, :].astype(F32).reshape(cb * 8, width)
    rows = pl.ds(pl.multiple_of((faces - cb) * high, cb), cb)
    total[rows, :] += dot(wide[pl.ds(0, cb, stride=8), :].astype(BF16), coupling[3 + high])


def edges_body(base, coupling, a_far, b_far, b_near, total, wide):
    faces, width = base.shape
    ca = b_far.shape[0] - 1
    cb = faces // ca
    odd_b = lax.axis_index("gy") % 2 == 1
    total[...] = base[...]
    gx_edge(total, a_far, wide, coupling, lax.axis_index("gx") % 2)
    for k, halo in enumerate((b_far, b_near)):
        wide[k * ca * 8:(k + 1) * ca * 8] = halo[0:ca, 0:8, :].astype(F32).reshape(ca * 8, width)

    def edge(k):
        own, other = (wide[pl.ds(n * ca * 8, ca, stride=8), :] for n in (k, 1 - k))
        return jnp.where(odd_b, other, own).astype(BF16)

    total[pl.ds(0, ca, stride=cb), :] += dot(edge(0), coupling[5])
    total[pl.ds(cb - 1, ca, stride=cb), :] += dot(edge(1), coupling[6])


def message_body(partial, pick, ids, coupling, a_far, a_near, out, total, wide):
    faces, width = partial.shape
    owners, slots = out.shape[0], faces // out.shape[0]
    cb = a_far.shape[0] - 2
    here = lax.axis_index("gy")
    odd_a = lax.axis_index("gx") % 2 == 1
    total[...] = partial[...]
    gx_edge(total, a_near, wide, coupling, 1 - lax.axis_index("gx") % 2)
    picked = dot(pick[...], total[...].astype(BF16)).astype(BF16)
    pb = a_far.shape[1]
    top = jnp.where(odd_a, a_near[cb + 1].astype(F32), a_far[cb + 1].astype(F32))
    bottom = jnp.where(odd_a, a_far[cb].astype(F32), a_near[cb].astype(F32))
    sub = lax.broadcasted_iota(jnp.int32, (MSG - slots, width), 0)

    def extra(o, column):
        rows = jnp.where(sub == 0, ids[o:o + 1, :], 0.0)
        rows = jnp.where(sub == 1, top[column:column + 1, :], rows)
        return jnp.where(sub == 2, bottom[column:column + 1, :], rows)

    for o in range(owners):
        out[o, 0:slots // 2] = picked[o * slots:(o + 1) * slots].reshape(slots // 2, 2, width)
        rest = jnp.where(o > here, extra(o, pb - 1), extra(o, 0)).astype(BF16)
        out[o, slots // 2:MSG // 2] = rest.reshape((MSG - slots) // 2, 2, width)


def update_body(adj, coupling, logf, a_far, a_near, b_far, b_near, out, prior, scale,
                a_lo, a_hi, b_lo, b_hi, held, field, once, sems):
    ca, cb, nl, width = adj.shape
    rows = cb * nl
    layer = lax.broadcasted_iota(jnp.int32, (rows, width), 0) % nl
    for axis, far, near, lo, hi in (
        ("gx", a_far, a_near, a_lo, a_hi), ("gy", b_far, b_near, b_lo, b_hi)
    ):
        odd = lax.axis_index(axis) % 2 == 1
        for which, low, high in ((odd, near, far), (jnp.logical_not(odd), far, near)):

            @pl.when(which)
            def _():
                lo[...] = low[...]
                hi[...] = high[...]

    copies = []
    for a in range(ca):
        own = adj[a].reshape(rows, width)
        down = adj[a - 1] if a > 0 else a_lo[0:cb]
        up = adj[a + 1] if a < ca - 1 else a_hi[0:cb]
        total = dot(own, coupling[0])
        below = pltpu.roll(dot(own, coupling[1]), 1, 0)
        above = pltpu.roll(dot(own, coupling[2]), rows - 1, 0)
        total = total + jnp.where(layer > 0, below, 0.0) + jnp.where(layer < nl - 1, above, 0.0)
        total = total + dot(down.reshape(rows, width), coupling[3])
        total = total + dot(up.reshape(rows, width), coupling[4])
        before = jnp.concatenate([b_lo[a], own[:rows - nl]], axis=0)
        behind = jnp.concatenate([own[nl:], b_hi[a]], axis=0)
        total = total + dot(before, coupling[5]) + dot(behind, coupling[6])
        held[a] = total.astype(BF16).reshape(cb, nl, width)
        copy = pltpu.make_async_copy(held.at[a], out.at[a], sems.at[a])
        copy.start()
        copies.append(copy)
    pa, pb = logf.shape[0], logf.shape[1]
    off = 8
    field[...] = jnp.zeros(field.shape, F32)
    field[2:pa + 2, off:off + pb] = logf[...]
    field[0:2, off:off + pb] = a_lo[cb:cb + 2].astype(F32)
    field[pa + 2:pa + 4, off:off + pb] = a_hi[cb:cb + 2].astype(F32)
    side_lo, side_hi = b_lo[ca].astype(F32), b_hi[ca].astype(F32)
    for r in range(pa):
        for c in range(2):
            field[r + 2, off - 2 + c:off - 1 + c] = side_lo[c * pa + r:c * pa + r + 1]
            field[r + 2, off + pb + c:off + pb + c + 1] = side_hi[c * pa + r:c * pa + r + 1]

    def stencil(ref, a, b, na, nb):
        beside = ref[a + 1:a + 1 + na, b:b + nb] + ref[a - 1:a - 1 + na, b:b + nb]
        beside = beside + ref[a:a + na, b + 1:b + 1 + nb] + ref[a:a + na, b - 1:b - 1 + nb]
        return 1.3 * ref[a:a + na, b:b + nb] - 0.2 * beside

    i, j = lax.axis_index("gx"), lax.axis_index("gy")
    last_i, last_j = lax.axis_size("gx") - 1, lax.axis_size("gy") - 1
    once[...] = jnp.zeros(once.shape, F32)
    once[1:pa + 1, off:off + pb] = stencil(field, 2, off, pa, pb)
    once[0:1, off:off + pb] = jnp.where(i > 0, stencil(field, 1, off, 1, pb), 0.0)
    once[pa + 1:pa + 2, off:off + pb] = jnp.where(i < last_i, stencil(field, pa + 2, off, 1, pb), 0.0)
    once[1:pa + 1, off - 1:off] = jnp.where(j > 0, stencil(field, 2, off - 1, pa, 1), 0.0)
    once[1:pa + 1, off + pb:off + pb + 1] = jnp.where(j < last_j, stencil(field, 2, off + pb, pa, 1), 0.0)
    prior[...] = stencil(once, 1, off, pa, pb)
    scale[...] = jnp.exp(logf[...])
    for copy in copies:
        copy.wait()


def gradient_body(got, prior, scale, out):
    owners, _, _, width = got.shape
    pa, pb, _ = out.shape
    slots = 16
    per_row = width // slots
    tail = got[:, slots // 2:MSG // 2].reshape(owners, MSG - slots, width).astype(F32)
    listed = [jnp.sum(tail[k:k + per_row], axis=0)[0:1] for k in range(0, owners, per_row)]
    listed = jnp.concatenate(listed, axis=1)
    node = lax.broadcasted_iota(jnp.int32, (pa * pb, owners * slots), 0).astype(F32) + 1.0
    onehot = jnp.where(node == listed, 1.0, 0.0).astype(BF16)
    blocks = got[:, 0:slots // 2].reshape(owners * slots, width)
    misfit = dot(onehot, blocks).reshape(pa, pb, width)
    out[...] = scale[...] * misfit + prior[...]
    j = lax.axis_index("gy")
    for side, column in ((-1, 0), (1, pb - 1)):
        inside = jnp.logical_and(j + side >= 0, j + side < owners)
        source = jnp.clip(j + side, 0, owners - 1)
        corners = jnp.where(inside, got[source, slots // 2:MSG // 2].reshape(MSG - slots, width).astype(F32) * 0.08, 0.0)
        out[0, column:column + 1] += corners[1:2]
        out[pa - 1, column:column + 1] += corners[2:3]


def cost(flops, size):
    return pl.CostEstimate(flops=flops, bytes_accessed=size, transcendentals=0)


def per_device(adjoint_trace, coupling, log_friction, send_column, live_count, target_node):
    ca, cb, nl, width = adjoint_trace.shape
    pa, pb, _ = log_friction.shape
    owners = lax.axis_size("gy")
    faces = ca * cb
    shape = jax.ShapeDtypeStruct
    wire = pltpu.CompilerParams(vmem_limit_bytes=16 * 2**20)

    to_a_far, to_a_near, to_b_far, to_b_near = pl.pallas_call(
        pack_body,
        out_shape=(
            shape((cb + 2, nl, width), BF16),
            shape((cb + 2, nl, width), BF16),
            shape((ca + 1, nl, width), BF16),
            shape((ca + 1, nl, width), BF16),
        ),
        in_specs=[HBM] * 2,
        out_specs=(VMEM,) * 4,
        scratch_shapes=[pltpu.VMEM(log_friction.shape, F32), pltpu.SemaphoreType.DMA((5,))],
        compiler_params=wire,
        cost_estimate=cost(10**9, 3 * 2**20),
        name="pack",
    )(in_hbm(adjoint_trace), in_hbm(log_friction))
    a_near = swap(to_a_near, "gx", 0)
    a_far = swap(to_a_far, "gx", 1)
    b_far = swap(to_b_far, "gy", 1)
    b_near = swap(to_b_near, "gy", 0)

    base, pick, ids = pl.pallas_call(
        local_body,
        out_shape=(
            shape((faces, width), F32),
            shape((faces, faces), BF16),
            shape((owners, width), F32),
        ),
        in_specs=[VMEM] * 5,
        out_specs=(VMEM,) * 3,
        scratch_shapes=[pltpu.VMEM((faces * 8, width), F32)],
        compiler_params=wire,
        cost_estimate=cost(2 * 6 * faces * width * width, 2 * 2**20),
        name="local",
    )(adjoint_trace, coupling, send_column, live_count, target_node)

    partial = pl.pallas_call(
        edges_body,
        out_shape=shape((faces, width), F32),
        in_specs=[VMEM] * 5,
        out_specs=VMEM,
        scratch_shapes=[pltpu.VMEM((2 * ca * 8, width), F32)],
        compiler_params=wire,
        cost_estimate=cost(2 * 3 * ca * width * width, 2**18),
        name="edges",
    )(base, coupling, a_far, b_far, b_near)

    message = pl.pallas_call(
        message_body,
        out_shape=shape((owners, MSG // 2, 2, width), BF16),
        in_specs=[VMEM] * 6,
        out_specs=VMEM,
        scratch_shapes=[
            pltpu.VMEM((faces, width), F32),
            pltpu.VMEM((cb * 8, width), F32),
        ],
        compiler_params=wire,
        cost_estimate=cost(2 * faces * faces * width, 2**20),
        name="message",
    )(partial, pick, ids, coupling, a_far, a_near)

    received = lax.all_to_all(message, "gy", split_axis=0, concat_axis=0, tiled=True)

    update, prior, scale = pl.pallas_call(
        update_body,
        out_shape=(
            shape(adjoint_trace.shape, BF16),
            shape(log_friction.shape, F32),
            shape(log_friction.shape, F32),
        ),
        in_specs=[VMEM] * 7,
        out_specs=(HBM, VMEM, VMEM),
        scratch_shapes=[
            pltpu.VMEM((cb + 2, nl, width), BF16),
            pltpu.VMEM((cb + 2, nl, width), BF16),
            pltpu.VMEM((ca + 1, nl, width), BF16),
            pltpu.VMEM((ca + 1, nl, width), BF16),
            pltpu.VMEM(adjoint_trace.shape, BF16),
            pltpu.VMEM((pa + 4, pb + 16, width), F32),
            pltpu.VMEM((pa + 2, pb + 16, width), F32),
            pltpu.SemaphoreType.DMA((ca,)),
        ],
        compiler_params=wire,
        cost_estimate=cost(2 * 7 * faces * nl * width * width, 4 * 2**20),
        name="update",
    )(adjoint_trace, coupling, log_friction, a_far, a_near, b_far, b_near)

    gradient = pl.pallas_call(
        gradient_body,
        out_shape=shape(log_friction.shape, F32),
        in_specs=[VMEM] * 3,
        out_specs=VMEM,
        compiler_params=wire,
        cost_estimate=cost(2 * pa * pb * faces * width, 2**19),
        name="gradient",
    )(received, prior, scale)
    return update, gradient


def solution(mesh):
    in_specs = (
        P("gx", "gy", None, None),
        P(),
        P("gx", "gy", None),
        P("gx", "gy", None),
        P("gx", "gy", None),
        P("gx", "gy", None, None),
    )
    out_specs = (P("gx", "gy", None, None), P("gx", "gy", None))
    return jax.shard_map(
        per_device, mesh=mesh, in_specs=in_specs, out_specs=out_specs, check_vma=False
    )
```
